256 devices in a mesh: gx: 32 (over x_hi, z, core), gy: 8 (over x_lo, y).
Axes of the slice: x: 4 (x_hi: 2, x_lo: 2; x = x_hi * 2 + x_lo), y: 4, z: 8, core: 2. Of those that a mesh axis runs over, the one named last changes fastest.
Arguments:
- background: bfloat16 [2, 2048, 1024, 128], P(None, 'gx', 'gy'), may hold values from -6 to 6
- observation_cell_index: int32 [32, 8, 512], P('gx', 'gy'), may hold values from 0 to 16383
- obs_value: float32 [32, 8, 512], P('gx', 'gy'), may hold values from -6 to 6
- obs_inverse: float32 [32, 8, 512], P('gx', 'gy'), may hold values from 0.5 to 4
- obs_count: int32 [32, 8], P('gx', 'gy'), may hold values from 256 to 512, as said below
- taper: int32 [64], replicated, may hold values from 32 to 1024
Outputs:
- analysis: bfloat16 [2, 2048, 1024, 128], P(None, 'gx', 'gy')
The draws below stay inside these ranges and needn't reach their ends.
Inputs may be any that keep to these rules, and one draw needn't show every extreme that they name: `obs_count`: some tile has exactly 512 live slots and some tile exactly 256.
All inputs are finite; a program needn't handle non-finite values.
Results may differ from the reference program's by a relative error of at most 0.0028.
The reference program's roundings to bfloat16 on the way count: a program that leaves them out, or rounds other values in their place, can miss the bound.
Values may be sent and summed in bfloat16 or wider, within the bound.
A program may use at most 64 MiB of HBM per device.

```python
import math
import jax
import jax.numpy as jnp
from jax import lax

K = 128
LEV = 2
TX = 64
TY = 128
OBS = 512
BINS = 64
NSTEPS = 6
TCOLS = 32
TROWS = 8
NX = 2048
NY = 1024
N_GX = 32
N_GY = 8


def draw_obs_count(key, part):
    first, second, third = jax.random.split(key, 3)
    draws_first = jax.random.randint(first, (TCOLS, TROWS), 1, OBS + 1)
    draws_second = jax.random.randint(second, (TCOLS, TROWS), 1, OBS + 1)
    skewed = OBS // 2 + draws_first * draws_second // (2 * OBS)
    skewed = jnp.minimum(skewed, OBS)
    chosen = jax.random.randint(third, (), 0, TCOLS * TROWS)
    lowest = (chosen + 1) % (TCOLS * TROWS)
    flat_ids = jnp.arange(TCOLS * TROWS, dtype=jnp.int32).reshape(TCOLS, TROWS)
    counts = jnp.where(flat_ids == lowest, OBS // 2, skewed)
    return jnp.where(flat_ids == chosen, OBS, counts).astype(jnp.int32)


def plant(values, rng, smallest, top_value):
    spot = [jax.random.randint(jax.random.fold_in(rng, axis), (), 0, length) for axis, length in enumerate(values.shape)]
    longest = values.shape.index(max(values.shape))
    neighbour = spot[:longest] + [(spot[longest] + 1) % values.shape[longest]] + spot[longest + 1:]
    return values.at[tuple(spot)].set(smallest).at[tuple(neighbour)].set(top_value)


def level_of(stream_key, extent, cuts, low, largest):
    def one(dim, shards_of):
        steps = jax.random.uniform(jax.random.fold_in(jax.random.fold_in(stream_key, 6), dim), (shards_of,), jnp.float32, low / len(cuts), largest / len(cuts))
        return jnp.repeat(jnp.exp(steps), extent[dim] // shards_of).reshape((-1,) + (1,) * (len(extent) - dim - 1))

    level = one(*cuts[0])
    for cut in cuts[1:]:
        level = level * one(*cut)
    return level


def noise(key, dims, width, most, cuts=(), held_as=jnp.bfloat16):
    array = jax.random.normal(key, dims, jnp.float32) * width
    if len(cuts) > 0:
        array = level_of(key, dims, cuts, -0.22, 0.18) * array
    return jnp.clip(array, min=-most, max=most).astype(held_as)


def setup_inputs(seed: int = 0) -> dict:
    arg_keys = jax.random.split(jax.random.key(seed), 7)
    return {
        "background": noise(arg_keys[0], (LEV, NX, NY, K), 1.0, 6.0, ((1, 32), (2, 8))),
        "observation_cell_index": plant(jax.random.randint(arg_keys[1], (TCOLS, TROWS, OBS), 0, LEV * TX * TY), jax.random.fold_in(arg_keys[1], 1), 0, (LEV * TX * TY) - 1).astype(jnp.int32),
        "obs_value": noise(arg_keys[2], (TCOLS, TROWS, OBS), 1.0, 6.0, ((0, 32), (1, 8)), jnp.float32),
        "obs_inverse": jnp.clip(jnp.exp(math.log(4.0) - 2.0794415 * jax.random.uniform(arg_keys[3], (TCOLS, TROWS, OBS), jnp.float32) ** level_of(arg_keys[3], (TCOLS, TROWS, OBS), ((0, 32), (1, 8)), -0.2, 0.2)), 0.5, 4.0),
        "obs_count": draw_obs_count(jax.random.fold_in(arg_keys[6], 71), 0),
        "taper": plant(jax.random.randint(arg_keys[5], (BINS,), 32, 1025), jax.random.fold_in(arg_keys[5], 1), 32, 1024).astype(jnp.int32),
    }


HIGH = lax.Precision.HIGHEST

def observe(ensemble, cell_ids, values, inverse, live_count, tile_x, tile_y):
    picked = jnp.take(ensemble, cell_ids, axis=0).astype(jnp.float32)
    center = lax.optimization_barrier(jnp.mean(picked, axis=1))
    perturb = (picked - center[:, None]).astype(jnp.bfloat16)
    slot_ids = jnp.arange(cell_ids.shape[0], dtype=jnp.int32)
    live_mask = (slot_ids < live_count).astype(jnp.float32)
    column_pos = cell_ids % (tile_x * tile_y) // tile_y
    row_pos = cell_ids % tile_y
    metadata = jnp.stack([values - center, inverse * live_mask, column_pos.astype(jnp.float32), row_pos.astype(jnp.float32)]).astype(jnp.bfloat16)
    return (perturb, metadata, live_mask)

def statistics(perturb, metadata, live_mask):
    members = perturb.shape[1]
    weight = metadata[1].astype(jnp.float32)
    innovation = metadata[0].astype(jnp.float32)
    spread = lax.optimization_barrier(jnp.sum(jnp.square(perturb.astype(jnp.float32)), axis=1)) / (members - 1)
    return (jnp.sum(weight * innovation * innovation), jnp.sum(weight * spread) + jnp.sum(live_mask))

def transform(perturb9, metadata9, inflation, taper, tile_x, tile_y):
    members = perturb9.shape[-1]
    bins = taper.shape[0]
    offsets = jnp.arange(3, dtype=jnp.int32) - 1
    column_pos = offsets[:, None, None] * tile_x + metadata9[:, :, 2, :].astype(jnp.int32)
    row_pos = offsets[None, :, None] * tile_y + metadata9[:, :, 3, :].astype(jnp.int32)
    delta_x = 2 * column_pos - (tile_x - 1)
    delta_y = 2 * row_pos - (tile_y - 1)
    distance = (delta_x * delta_x + delta_y * delta_y) * bins
    limit = 9 * (tile_x * tile_x + tile_y * tile_y)
    bin_edges = jnp.arange(bins, dtype=jnp.int32) * limit
    in_bin = (distance[..., None] >= bin_edges) & (distance[..., None] < bin_edges + limit)
    tapered_weight_factor = lax.optimization_barrier(jnp.sum(jnp.where(in_bin, taper.astype(jnp.float32), jnp.float32(0.0)), axis=-1)) / 1024.0
    effective = metadata9[:, :, 1, :].astype(jnp.float32) * tapered_weight_factor
    flat = perturb9.reshape(-1, members)
    weighted = (flat.astype(jnp.float32) * effective.reshape(-1)[:, None]).astype(jnp.bfloat16)
    gram_matrix = lax.dot_general(weighted, flat, (((0,), (0,)), ((), ())), preferred_element_type=jnp.float32)
    innovation = metadata9[:, :, 0, :].reshape(1, -1)
    projected = jnp.dot(innovation, weighted, preferred_element_type=jnp.float32)[0]
    identity = jnp.eye(members, dtype=jnp.float32)
    system = identity / inflation + gram_matrix / (members - 1)
    frobenius = jnp.sqrt(jnp.sum(system * system))
    root_iter = system / frobenius
    inverse_root = identity
    for sweep in range(NSTEPS):
        correction = 1.5 * identity - 0.5 * jnp.dot(inverse_root, root_iter, precision=HIGH, preferred_element_type=jnp.float32)
        root_iter = jnp.dot(root_iter, correction, precision=HIGH, preferred_element_type=jnp.float32)
        inverse_root = jnp.dot(correction, inverse_root, precision=HIGH, preferred_element_type=jnp.float32)
    spread_weights = inverse_root / jnp.sqrt(frobenius)
    inner = jnp.dot(inverse_root, projected, precision=HIGH, preferred_element_type=jnp.float32)
    mean_weights = jnp.dot(inverse_root, inner, precision=HIGH, preferred_element_type=jnp.float32) / (frobenius * (members - 1))
    return (spread_weights + mean_weights[:, None]).astype(jnp.bfloat16)

def spline(length, tile_id, tiles):
    position = (jnp.arange(length, dtype=jnp.float32) + 0.5) / length
    left_part = 0.5 * jnp.square(1.0 - position)
    middle = 0.5 + position - jnp.square(position)
    right_part = 0.5 * jnp.square(position)
    has_left = (tile_id > 0).astype(jnp.float32)
    has_right = (tile_id < tiles - 1).astype(jnp.float32)
    middle = middle + (1.0 - has_left) * left_part + (1.0 - has_right) * right_part
    return jnp.stack([left_part * has_left, middle, right_part * has_right])

def blend(ensemble, weights9, column_id, row_id, columns, row_tiles):
    levels, tile_x, tile_y, members = ensemble.shape
    widened = ensemble.astype(jnp.float32)
    center = lax.optimization_barrier(jnp.mean(widened, axis=-1, keepdims=True))
    deviation = widened - center
    beta_x = spline(tile_x, column_id, columns)
    beta_y = spline(tile_y, row_id, row_tiles)
    analysis = center
    for offset_y in range(3):
        pieces = [(deviation * (beta_x[offset_x][:, None] * beta_y[offset_y][None, :])[None, :, :, None]).astype(jnp.bfloat16) for offset_x in range(3)]
        stacked = jnp.concatenate(pieces, axis=-1).reshape(-1, 3 * members)
        column_stack = weights9[:, offset_y].reshape(3 * members, members)
        product = jnp.dot(stacked, column_stack, preferred_element_type=jnp.float32)
        analysis = analysis + product.reshape(levels, tile_x, tile_y, members)
    return analysis.astype(jnp.bfloat16)

def reference(background, observation_cell_index, obs_value, obs_inverse, obs_count, taper):
    tiles = background.reshape(LEV, N_GX, TX, N_GY, TY, K).transpose(1, 3, 0, 2, 4, 5)
    tiles = tiles.reshape(N_GX * N_GY, LEV, TX, TY, K)

    def observe_tile(kernel_arguments):
        tile_state, cell_ids, values, inverse, live_count = kernel_arguments
        perturb, metadata, live_mask = observe(tile_state.reshape(-1, K), cell_ids, values, inverse, live_count, TX, TY)
        numerator, denominator = statistics(perturb, metadata, live_mask)
        return (perturb, metadata, numerator, denominator)
    perturb, metadata, numerators, denominators = lax.map(observe_tile, (tiles, observation_cell_index.reshape(-1, OBS), obs_value.reshape(-1, OBS), obs_inverse.reshape(-1, OBS), obs_count.reshape(-1)))
    inflation = jnp.sum(numerators) / jnp.sum(denominators)
    padded_pert = jnp.pad(perturb.reshape(N_GX, N_GY, OBS, K), ((1, 1), (1, 1), (0, 0), (0, 0)))
    padded_meta = jnp.pad(metadata.reshape(N_GX, N_GY, 4, OBS), ((1, 1), (1, 1), (0, 0), (0, 0)))
    zero_index = jnp.zeros((), jnp.int32)

    def weigh_tile(tile_id):
        column_id = (tile_id // N_GY).astype(jnp.int32)
        row_id = (tile_id % N_GY).astype(jnp.int32)
        neighbour_perturbation_rows = lax.dynamic_slice(padded_pert, (column_id, row_id, zero_index, zero_index), (3, 3, OBS, K))
        neighbour_metadata_rows = lax.dynamic_slice(padded_meta, (column_id, row_id, zero_index, zero_index), (3, 3, 4, OBS))
        return transform(neighbour_perturbation_rows, neighbour_metadata_rows, inflation, taper, TX, TY)
    tile_ids = jnp.arange(N_GX * N_GY, dtype=jnp.int32)
    weights = lax.map(weigh_tile, tile_ids).reshape(N_GX, N_GY, K, K)
    padded_weights = jnp.pad(weights, ((1, 1), (1, 1), (0, 0), (0, 0)))

    def blend_tile(kernel_arguments):
        tile_id, tile_state = kernel_arguments
        column_id = (tile_id // N_GY).astype(jnp.int32)
        row_id = (tile_id % N_GY).astype(jnp.int32)
        near_weights = lax.dynamic_slice(padded_weights, (column_id, row_id, zero_index, zero_index), (3, 3, K, K))
        return blend(tile_state, near_weights, column_id, row_id, N_GX, N_GY)
    result = lax.map(blend_tile, (tile_ids, tiles))
    result = result.reshape(N_GX, N_GY, LEV, TX, TY, K).transpose(2, 0, 3, 1, 4, 5)
    return result.reshape(LEV, N_GX * TX, N_GY * TY, K)
```

```python
import functools

import jax
import jax.numpy as jnp
from jax import lax
from jax.experimental import pallas as pl
from jax.experimental.pallas import tpu as pltpu
from jax.sharding import PartitionSpec as P

NSTEPS = 6
HIGH = lax.Precision.HIGHEST
MESH = pl.DeviceIdType.MESH
F32 = jnp.float32
BF16 = jnp.bfloat16

K = 128
OBS = 512
TX = 64
TY = 128
BINS = 64
LIMIT = 9 * (TX * TX + TY * TY)
CELLS = 2 * TX * TY
LOADS = 8
GROWS = K + 8
BLOCK = 16


def nt(a, b):
    return lax.dot_general(a, b, (((1,), (1,)), ((), ())), preferred_element_type=F32)


def mm(a, b):
    return jnp.dot(a, b, preferred_element_type=F32)


def high(a, b):
    return jnp.dot(a, b, precision=HIGH, preferred_element_type=F32)


def beta(position, has_low, has_high):
    low = 0.5 * ((1.0 - position) * (1.0 - position))
    middle = 0.5 + position - position * position
    top = 0.5 * (position * position)
    middle = middle + (1.0 - has_low) * low + (1.0 - has_high) * top
    return low * has_low, middle, top * has_high


def kernel(
    n_gx,
    n_gy,
    field,
    cell_s,
    cell_v,
    value,
    inverse,
    count,
    taper,
    out,
    field_v,
    acc,
    s_own,
    u_side,
    t_mid,
    t_ends,
    by_tab,
    picked,
    weighted,
    rhs,
    gram,
    gram_x,
    half,
    gram_y,
    sum_a,
    sum_b,
    w_all,
    load_sem,
    send_a,
    recv_a,
    send_b,
    recv_b,
    send_gx,
    recv_gx,
    send_gy,
    recv_gy,
    send_wy,
    recv_wy,
    send_wx,
    recv_wx,
    send_wc,
    recv_wc,
):
    gx = lax.axis_index("gx")
    gy = lax.axis_index("gy")
    span = CELLS // LOADS
    loads = [
        pltpu.make_async_copy(
            field.at[pl.ds(k * span, span), :], field_v.at[pl.ds(k * span, span), :], load_sem.at[k]
        )
        for k in range(LOADS)
    ]
    for load in loads:
        load.start()

    gram_x[...] = jnp.zeros_like(gram_x)
    gram_y[...] = jnp.zeros_like(gram_y)
    w_all[...] = jnp.zeros_like(w_all)

    block = lax.div(gx, BLOCK)
    lane = lax.rem(gx, BLOCK)
    plane = block * n_gy + gy
    planes = n_gx // BLOCK * n_gy

    def ring_peer(k):
        return (block * BLOCK + lax.rem(lane + k, BLOCK), gy)

    def plane_peer(k):
        other = lax.rem(plane + k, planes)
        return (lax.div(other, n_gy) * BLOCK + lane, lax.rem(other, n_gy))

    west, east = gx > 0, gx < n_gx - 1
    south, north = gy > 0, gy < n_gy - 1
    sides = [
        (west, (gx - 1, gy)),
        (east, (gx + 1, gy)),
        (south, (gx, gy - 1)),
        (north, (gx, gy + 1)),
    ]

    barrier = pltpu.get_barrier_semaphore()
    for k in range(1, BLOCK):
        pl.semaphore_signal(barrier, inc=1, device_id=ring_peer(k), device_id_type=MESH)
    for k in range(1, planes):
        pl.semaphore_signal(barrier, inc=1, device_id=plane_peer(k), device_id_type=MESH)
    for there, peer in sides:

        @pl.when(there)
        def _(peer=peer):
            pl.semaphore_signal(barrier, inc=1, device_id=peer, device_id_type=MESH)

    cells = cell_v[...]
    col = lax.shift_right_logical(cells & (TX * TY - 1), 7)
    row = cells & (TY - 1)
    slot = lax.broadcasted_iota(jnp.int32, (1, OBS), 1)
    live = (slot < count[0, 0]).astype(F32)
    weight = (inverse[...] * live).astype(BF16).astype(F32)
    which = lax.broadcasted_iota(jnp.int32, (BLOCK, OBS), 0)
    third = lax.shift_right_logical(which * 11, 5)
    dx = 2 * ((third - 1) * TX + col) - (TX - 1)
    dy = 2 * ((which - third * 3 - 1) * TY + row) - (TY - 1)
    distance = (dx * dx + dy * dy) * BINS
    factor = jnp.zeros((BLOCK, OBS), F32)
    for n in range(BINS):
        factor = jnp.where(distance >= n * LIMIT, taper[0, n].astype(F32), factor)
    effective = weight * (factor / 1024.0)

    has_s, has_n = south.astype(F32), north.astype(F32)
    has_w, has_e = west.astype(F32), east.astype(F32)
    v_pos = (lax.broadcasted_iota(jnp.int32, (TY, K), 0).astype(F32) + 0.5) / TY
    for q, part in enumerate(beta(v_pos, has_s, has_n)):
        by_tab[q] = part

    def beta_x(li):
        return beta(((li & (TX - 1)).astype(F32) + 0.5) / TX, has_w, has_e)

    for k in range(LOADS):
        loads[k].wait()

        def widen(i, _, k=k):
            rows = pl.ds(pl.multiple_of(k * span + i * 256, 256), 256)
            acc[rows, :] = field_v[rows, :].astype(F32)
            return 0

        lax.fori_loop(0, span // 256, widen, 0, unroll=True)

    def pick(i, _):
        for k in range(16):
            s = i * 16 + k
            picked[pl.ds(s, 1), :] = acc[pl.ds(cell_s[0, s], 1), :]
        return 0

    lax.fori_loop(0, OBS // 16, pick, 0)

    mean = jnp.full((K, K), 1.0 / K, BF16)
    cols = lax.broadcasted_iota(jnp.int32, (K, K), 1)
    rows_ = lax.broadcasted_iota(jnp.int32, (K, K), 0)
    eye = (cols == rows_).astype(F32)
    chosen = picked[...]
    chosen_b = chosen.astype(BF16)
    center_b = mm(chosen_b, mean)
    center_r = nt(mean[:16], chosen_b)[:1]
    perturb = (chosen - center_b).astype(BF16)
    perturb_t = nt(eye.astype(BF16), perturb)
    innovation = (value[...] - center_r).astype(BF16).astype(F32)
    spread = jnp.sum(perturb_t * perturb_t, axis=0, keepdims=True) / (K - 1)
    num = weight * innovation * innovation
    den = weight * spread + live
    num = num[:, :K] + num[:, K : 2 * K] + num[:, 2 * K : 3 * K] + num[:, 3 * K :]
    den = den[:, :K] + den[:, K : 2 * K] + den[:, 2 * K : 3 * K] + den[:, 3 * K :]
    num = num + pltpu.roll(num, K // 2, 1)
    den = den + pltpu.roll(den, K // 2, 1)
    lanes = lax.broadcasted_iota(jnp.int32, (1, K), 1)
    sum_a[0] = jnp.where(lanes < K // 2, num, den)

    pl.semaphore_wait(
        barrier,
        BLOCK - 1
        + planes - 1
        + west.astype(jnp.int32)
        + east.astype(jnp.int32)
        + south.astype(jnp.int32)
        + north.astype(jnp.int32),
    )

    def remote(src, dst, send, recv, peer):
        return pltpu.make_async_remote_copy(
            src_ref=src, dst_ref=dst, send_sem=send, recv_sem=recv, device_id=peer, device_id_type=MESH
        )

    ring = [
        remote(sum_a.at[0], sum_a.at[k], send_a.at[k], recv_a.at[k], ring_peer(k))
        for k in range(1, BLOCK)
    ]
    for copy in ring:
        copy.start()

    rhs[:, :K] = perturb
    d_rows = jnp.broadcast_to(innovation, (K, OBS)).T
    rhs[:, K:] = d_rows.astype(BF16)
    for t in range(9):
        weighted[t * K : (t + 1) * K, :] = (perturb_t * effective[t : t + 1, :]).astype(BF16)
    right = rhs[...]
    for t in range(9):
        product = mm(weighted[t * K : (t + 1) * K, :], right)
        gram[t, :K, :] = product[:, :K]
        gram[t, K:, :] = jnp.broadcast_to(
            jnp.sum(product[:, K:] * eye, axis=0, keepdims=True), (GROWS - K, K)
        )

    def for_sides(pairs, act):
        for there, copy in pairs:

            @pl.when(there)
            def _(copy=copy):
                act(copy)

    gx_out = [
        (east, remote(gram.at[pl.ds(0, 3)], gram_x.at[0], send_gx.at[0], recv_gx.at[0], (gx + 1, gy))),
        (west, remote(gram.at[pl.ds(6, 3)], gram_x.at[1], send_gx.at[1], recv_gx.at[1], (gx - 1, gy))),
    ]
    gx_in = [(west, gx_out[0][1]), (east, gx_out[1][1])]
    for_sides(gx_out, lambda copy: copy.start())

    lines = 4

    def prepare(c, _):
        size = lines * TY
        rows = pl.ds(pl.multiple_of(c * size, size), size)
        members = field_v[rows, :]
        center = mm(members, mean)
        acc[rows, :] = center
        deviation = members.astype(F32) - center
        low, middle, top = by_tab[0], by_tab[1], by_tab[2]
        for n in range(lines):
            _, bx, _ = beta_x(c * lines + n)
            piece = deviation[n * TY : (n + 1) * TY]
            at = pl.ds(pl.multiple_of(c * size + n * TY, TY), TY)
            t_ends[at, :K] = (piece * low).astype(BF16)
            t_ends[at, K:] = (piece * top).astype(BF16)
            t_mid[at, :] = (piece * middle).astype(BF16)
            u_side[at, :] = (piece * bx).astype(BF16)
            s_own[at, :] = (piece * (middle * bx)).astype(BF16)
        return 0

    steps = 2 * TX // lines
    lax.fori_loop(0, steps // 2, prepare, 0)

    for copy in ring:
        copy.wait_recv()
    sum_b[0] = jnp.sum(sum_a[...], axis=0)
    cross = [
        remote(sum_b.at[0], sum_b.at[k], send_b.at[k], recv_b.at[k], plane_peer(k))
        for k in range(1, planes)
    ]
    for copy in cross:
        copy.start()

    for_sides(gx_in, lambda copy: copy.wait_recv())
    half[0] = gram[3] + gram_x[0, 0] + gram_x[1, 0]
    half[1] = gram[5] + gram_x[0, 2] + gram_x[1, 2]
    gy_out = [
        (north, remote(half.at[0], gram_y.at[0], send_gy.at[0], recv_gy.at[0], (gx, gy + 1))),
        (south, remote(half.at[1], gram_y.at[1], send_gy.at[1], recv_gy.at[1], (gx, gy - 1))),
    ]
    gy_in = [(south, gy_out[0][1]), (north, gy_out[1][1])]
    for_sides(gy_out, lambda copy: copy.start())

    lax.fori_loop(steps // 2, steps, prepare, 0)

    for_sides(gy_in, lambda copy: copy.wait_recv())
    total = gram[4] + gram_x[0, 1] + gram_x[1, 1] + gram_y[0] + gram_y[1]
    projected = jnp.broadcast_to(total[K : K + 1], (K, K)).T
    total = total[:K]

    for copy in cross:
        copy.wait_recv()
    sums = jnp.sum(sum_b[...], axis=0)
    numerator = jnp.sum(jnp.where(lanes < K // 2, sums, 0.0), axis=1, keepdims=True)
    denominator = jnp.sum(jnp.where(lanes < K // 2, 0.0, sums), axis=1, keepdims=True)
    inflation = numerator / denominator

    system = eye / inflation + total / (K - 1)
    frob = jnp.sqrt(jnp.sum(jnp.sum(system * system, axis=0, keepdims=True), axis=1, keepdims=True))
    root = system / frob
    inv_root = None
    for sweep in range(NSTEPS):
        joint = root if sweep == 0 else high(inv_root, root)
        correction = 1.5 * eye - 0.5 * joint
        if sweep < NSTEPS - 1:
            root = high(root, correction)
        inv_root = correction if sweep == 0 else high(correction, inv_root)
    shift = high(inv_root, high(inv_root, projected)) / (frob * (K - 1))
    w_all[1, 1] = (inv_root / jnp.sqrt(frob) + shift).astype(BF16)

    mine = w_all.at[1, 1]
    wy_out = [
        (north, remote(mine, w_all.at[1, 0], send_wy.at[0], recv_wy.at[0], (gx, gy + 1))),
        (south, remote(mine, w_all.at[1, 2], send_wy.at[1], recv_wy.at[1], (gx, gy - 1))),
    ]
    wy_in = [(south, wy_out[0][1]), (north, wy_out[1][1])]
    wx_out = [
        (east, remote(mine, w_all.at[0, 1], send_wx.at[0], recv_wx.at[0], (gx + 1, gy))),
        (west, remote(mine, w_all.at[2, 1], send_wx.at[1], recv_wx.at[1], (gx - 1, gy))),
    ]
    wx_in = [(west, wx_out[0][1]), (east, wx_out[1][1])]
    for_sides(wy_out, lambda copy: copy.start())
    for_sides(wx_out, lambda copy: copy.start())

    wide = 8
    size = wide * TY

    def own(c, _):
        rows = pl.ds(pl.multiple_of(c * size, size), size)
        acc[rows, :] = acc[rows, :] + mm(s_own[rows, :], w_all[1, 1])
        return 0

    lax.fori_loop(0, CELLS // size, own, 0)

    for_sides(wy_in, lambda copy: copy.wait_recv())
    wc_out = []
    wc_in = []
    for n, (from_y, q) in enumerate(((south, 0), (north, 2))):
        to_e = remote(w_all.at[1, q], w_all.at[0, q], send_wc.at[0, n], recv_wc.at[0, n], (gx + 1, gy))
        to_w = remote(w_all.at[1, q], w_all.at[2, q], send_wc.at[1, n], recv_wc.at[1, n], (gx - 1, gy))
        wc_out += [(jnp.logical_and(from_y, east), to_e), (jnp.logical_and(from_y, west), to_w)]
        wc_in += [(jnp.logical_and(from_y, west), to_e), (jnp.logical_and(from_y, east), to_w)]
    for_sides(wc_out, lambda copy: copy.start())
    for_sides(wx_in, lambda copy: copy.wait_recv())

    def edges(c, _):
        rows = pl.ds(pl.multiple_of(c * size, size), size)
        along_x = mm(t_mid[rows, :], jnp.concatenate([w_all[0, 1], w_all[2, 1]], axis=1))
        along_y = mm(u_side[rows, :], jnp.concatenate([w_all[1, 0], w_all[1, 2]], axis=1))
        for n in range(wide):
            bl, _, bh = beta_x(c * wide + n)
            cut = slice(n * TY, (n + 1) * TY)
            at = pl.ds(pl.multiple_of(c * size + n * TY, TY), TY)
            acc[at, :] = (
                acc[at, :]
                + (bl * along_x[cut, :K] + bh * along_x[cut, K:])
                + (by_tab[0] * along_y[cut, :K] + by_tab[2] * along_y[cut, K:])
            )
        return 0

    lax.fori_loop(0, CELLS // size, edges, 0)

    for_sides(wc_in, lambda copy: copy.wait_recv())

    def corners(c, _):
        rows = pl.ds(pl.multiple_of(c * size, size), size)
        ends = jnp.concatenate(
            [
                jnp.concatenate([w_all[0, 0], w_all[2, 0]], axis=1),
                jnp.concatenate([w_all[0, 2], w_all[2, 2]], axis=1),
            ],
            axis=0,
        )
        product = mm(t_ends[rows, :], ends)
        for n in range(wide):
            bl, _, bh = beta_x(c * wide + n)
            cut = slice(n * TY, (n + 1) * TY)
            at = pl.ds(pl.multiple_of(c * size + n * TY, TY), TY)
            out[at, :] = (acc[at, :] + (bl * product[cut, :K] + bh * product[cut, K:])).astype(BF16)
        return 0

    lax.fori_loop(0, CELLS // size, corners, 0)

    for copy in ring + cross:
        copy.wait_send()
    for_sides(gx_out + gy_out + wy_out + wx_out + wc_out, lambda copy: copy.wait_send())


def local(n_gx, n_gy, background, cell_index, obs_value, obs_inverse, obs_count, taper):
    levels, tile_x, tile_y, members = background.shape
    field = background.reshape(-1, members)
    cells = cell_index.reshape(1, OBS)
    smem = pl.BlockSpec(memory_space=pltpu.SMEM)
    vmem = pl.BlockSpec(memory_space=pltpu.VMEM)
    dma = pltpu.SemaphoreType.DMA
    planes = n_gx // BLOCK * n_gy
    result = pl.pallas_call(
        functools.partial(kernel, n_gx, n_gy),
        out_shape=jax.ShapeDtypeStruct((CELLS, K), BF16),
        in_specs=[pl.BlockSpec(memory_space=pltpu.HBM), smem, vmem, vmem, vmem, smem, smem],
        out_specs=vmem,
        scratch_shapes=[
            pltpu.VMEM((CELLS, K), BF16),
            pltpu.VMEM((CELLS, K), F32),
            pltpu.VMEM((CELLS, K), BF16),
            pltpu.VMEM((CELLS, K), BF16),
            pltpu.VMEM((CELLS, K), BF16),
            pltpu.VMEM((CELLS, 2 * K), BF16),
            pltpu.VMEM((3, TY, K), F32),
            pltpu.VMEM((OBS, K), F32),
            pltpu.VMEM((9 * K, OBS), BF16),
            pltpu.VMEM((OBS, 2 * K), BF16),
            pltpu.VMEM((9, GROWS, K), F32),
            pltpu.VMEM((2, 3, GROWS, K), F32),
            pltpu.VMEM((2, GROWS, K), F32),
            pltpu.VMEM((2, GROWS, K), F32),
            pltpu.VMEM((BLOCK, 1, K), F32),
            pltpu.VMEM((planes, 1, K), F32),
            pltpu.VMEM((3, 3, K, K), BF16),
            dma((LOADS,)),
            dma((BLOCK,)),
            dma((BLOCK,)),
            dma((planes,)),
            dma((planes,)),
            dma((2,)),
            dma((2,)),
            dma((2,)),
            dma((2,)),
            dma((2,)),
            dma((2,)),
            dma((2,)),
            dma((2,)),
            dma((2, 2)),
            dma((2, 2)),
        ],
        compiler_params=pltpu.CompilerParams(
            collective_id=0, has_side_effects=True, vmem_limit_bytes=60 * 1024 * 1024
        ),
    )(
        field,
        cells,
        cells,
        obs_value.reshape(1, OBS),
        obs_inverse.reshape(1, OBS),
        obs_count.reshape(1, 1),
        taper.reshape(1, BINS),
    )
    return result.reshape(levels, tile_x, tile_y, members)


def solution(mesh):
    in_specs = (
        P(None, "gx", "gy", None),
        P("gx", "gy", None),
        P("gx", "gy", None),
        P("gx", "gy", None),
        P("gx", "gy"),
        P(),
    )
    out_specs = P(None, "gx", "gy", None)
    step = functools.partial(local, mesh.shape["gx"], mesh.shape["gy"])
    return jax.shard_map(step, mesh=mesh, in_specs=in_specs, out_specs=out_specs, check_vma=False)
```

```python
import functools

import jax
import jax.numpy as jnp
from jax import lax
from jax.experimental import pallas as pl
from jax.experimental.pallas import tpu as pltpu
from jax.sharding import PartitionSpec as P

NSTEPS = 6
HIGH = lax.Precision.HIGHEST
MESH = pl.DeviceIdType.MESH
F32 = jnp.float32
BF16 = jnp.bfloat16

K = 128
OBS = 512
TX = 64
TY = 128
BINS = 64
LIMIT = 9 * (TX * TX + TY * TY)
CELLS = 2 * TX * TY
LOADS = 8
GROWS = K + 8
BLOCK = 16


def nt(a, b):
    return lax.dot_general(a, b, (((1,), (1,)), ((), ())), preferred_element_type=F32)


def mm(a, b):
    return jnp.dot(a, b, preferred_element_type=F32)


def high(a, b):
    return jnp.dot(a, b, precision=HIGH, preferred_element_type=F32)


def beta(position, has_low, has_high):
    low = 0.5 * ((1.0 - position) * (1.0 - position))
    middle = 0.5 + position - position * position
    top = 0.5 * (position * position)
    middle = middle + (1.0 - has_low) * low + (1.0 - has_high) * top
    return low * has_low, middle, top * has_high


def by_line(table, p, line, x):
    return (x.reshape(TY // 8, 8, K) * table[p, line][None]).reshape(TY, K)


def last_pass(acc, scaled, sides_w, bx_tab, out, result, out_sem):
    size = 16 * TY
    copies = [
        pltpu.make_async_copy(
            result.at[pl.ds(c * size, size), :], out.at[pl.ds(c * size, size), :], out_sem.at[c]
        )
        for c in range(CELLS // size)
    ]

    for c in range(CELLS // size):
        product = mm(scaled[c * size : (c + 1) * size, :], sides_w[...])
        for n in range(size // TY):
            line = (c * (size // TY) + n) % TX
            cut = slice(n * TY, (n + 1) * TY)
            at = slice(c * size + n * TY, c * size + (n + 1) * TY)
            result[at, :] = (
                acc[at, :]
                + by_line(bx_tab, 0, line, product[cut, :K])
                + by_line(bx_tab, 2, line, product[cut, K:])
            ).astype(BF16)
        copies[c].start()
    for copy in copies:
        copy.wait()


def kernel(
    n_gx,
    n_gy,
    field,
    cell_s,
    cell_v,
    value,
    inverse,
    count,
    taper,
    acc,
    scaled,
    sides_w,
    bx_tab,
    field_v,
    s_own,
    u_side,
    by_tab,
    picked,
    weighted,
    rhs,
    gram,
    gram_x,
    half,
    gram_y,
    sum_a,
    sum_b,
    w_all,
    load_sem,
    send_a,
    recv_a,
    send_b,
    recv_b,
    send_gx,
    recv_gx,
    send_gy,
    recv_gy,
    send_wy,
    recv_wy,
    send_wx,
    recv_wx,
    send_wc,
    recv_wc,
):
    gx = lax.axis_index("gx")
    gy = lax.axis_index("gy")
    span = CELLS // LOADS
    loads = [
        pltpu.make_async_copy(
            field.at[pl.ds(k * span, span), :], field_v.at[pl.ds(k * span, span), :], load_sem.at[k]
        )
        for k in range(LOADS)
    ]
    for load in loads:
        load.start()

    gram_x[...] = jnp.zeros_like(gram_x)
    gram_y[...] = jnp.zeros_like(gram_y)
    w_all[...] = jnp.zeros_like(w_all)

    block = lax.div(gx, BLOCK)
    lane = lax.rem(gx, BLOCK)
    plane = block * n_gy + gy
    planes = n_gx // BLOCK * n_gy

    def ring_peer(k):
        return (block * BLOCK + lax.rem(lane + k, BLOCK), gy)

    def plane_peer(k):
        other = lax.rem(plane + k, planes)
        return (lax.div(other, n_gy) * BLOCK + lane, lax.rem(other, n_gy))

    west, east = gx > 0, gx < n_gx - 1
    south, north = gy > 0, gy < n_gy - 1
    sides = [
        (west, (gx - 1, gy)),
        (east, (gx + 1, gy)),
        (south, (gx, gy - 1)),
        (north, (gx, gy + 1)),
    ]

    barrier = pltpu.get_barrier_semaphore()
    for k in range(1, BLOCK):
        pl.semaphore_signal(barrier, inc=1, device_id=ring_peer(k), device_id_type=MESH)
    for k in range(1, planes):
        pl.semaphore_signal(barrier, inc=1, device_id=plane_peer(k), device_id_type=MESH)
    for there, peer in sides:

        @pl.when(there)
        def _(peer=peer):
            pl.semaphore_signal(barrier, inc=1, device_id=peer, device_id_type=MESH)

    cells = cell_v[...]
    col = lax.shift_right_logical(cells & (TX * TY - 1), 7)
    row = cells & (TY - 1)
    slot = lax.broadcasted_iota(jnp.int32, (1, OBS), 1)
    live = (slot < count[0, 0]).astype(F32)
    weight = (inverse[...] * live).astype(BF16).astype(F32)
    which = lax.broadcasted_iota(jnp.int32, (BLOCK, OBS), 0)
    third = lax.shift_right_logical(which * 11, 5)
    dx = 2 * ((third - 1) * TX + col) - (TX - 1)
    dy = 2 * ((which - third * 3 - 1) * TY + row) - (TY - 1)
    distance = (dx * dx + dy * dy) * BINS
    factor = jnp.zeros((BLOCK, OBS), F32)
    for n in range(BINS):
        factor = jnp.where(distance >= n * LIMIT, taper[0, n].astype(F32), factor)
    effective = weight * (factor / 1024.0)

    has_s, has_n = south.astype(F32), north.astype(F32)
    has_w, has_e = west.astype(F32), east.astype(F32)
    v_pos = (lax.broadcasted_iota(jnp.int32, (TY, K), 0).astype(F32) + 0.5) / TY
    for q, part in enumerate(beta(v_pos, has_s, has_n)):
        by_tab[q] = part

    u_pos = (lax.broadcasted_iota(jnp.int32, (TX, 8, K), 0).astype(F32) + 0.5) / TX
    for p, part in enumerate(beta(u_pos, has_w, has_e)):
        bx_tab[p] = part

    for k in range(LOADS):
        loads[k].wait()

        def widen(i, _, k=k):
            rows = pl.ds(pl.multiple_of(k * span + i * 256, 256), 256)
            acc[rows, :] = field_v[rows, :].astype(F32)
            return 0

        lax.fori_loop(0, span // 256, widen, 0, unroll=True)

    def pick(i, _):
        for k in range(16):
            s = i * 16 + k
            picked[pl.ds(s, 1), :] = acc[pl.ds(cell_s[0, s], 1), :]
        return 0

    lax.fori_loop(0, OBS // 16, pick, 0)

    mean = jnp.full((K, K), 1.0 / K, BF16)
    cols = lax.broadcasted_iota(jnp.int32, (K, K), 1)
    rows_ = lax.broadcasted_iota(jnp.int32, (K, K), 0)
    eye = (cols == rows_).astype(F32)
    chosen = picked[...]
    chosen_b = chosen.astype(BF16)
    center_b = mm(chosen_b, mean)
    center_r = nt(mean[:16], chosen_b)[:1]
    perturb = (chosen - center_b).astype(BF16)
    perturb_t = nt(eye.astype(BF16), perturb)
    innovation = (value[...] - center_r).astype(BF16).astype(F32)
    spread = jnp.sum(perturb_t * perturb_t, axis=0, keepdims=True) / (K - 1)
    num = weight * innovation * innovation
    den = weight * spread + live
    num = num[:, :K] + num[:, K : 2 * K] + num[:, 2 * K : 3 * K] + num[:, 3 * K :]
    den = den[:, :K] + den[:, K : 2 * K] + den[:, 2 * K : 3 * K] + den[:, 3 * K :]
    num = num + pltpu.roll(num, K // 2, 1)
    den = den + pltpu.roll(den, K // 2, 1)
    lanes = lax.broadcasted_iota(jnp.int32, (1, K), 1)
    sum_a[0] = jnp.where(lanes < K // 2, num, den)

    pl.semaphore_wait(
        barrier,
        BLOCK - 1
        + planes - 1
        + west.astype(jnp.int32)
        + east.astype(jnp.int32)
        + south.astype(jnp.int32)
        + north.astype(jnp.int32),
    )

    def remote(src, dst, send, recv, peer):
        return pltpu.make_async_remote_copy(
            src_ref=src, dst_ref=dst, send_sem=send, recv_sem=recv, device_id=peer, device_id_type=MESH
        )

    ring = [
        remote(sum_a.at[0], sum_a.at[k], send_a.at[k], recv_a.at[k], ring_peer(k))
        for k in range(1, BLOCK)
    ]
    for copy in ring:
        copy.start()

    rhs[:, :K] = perturb
    d_rows = jnp.broadcast_to(innovation, (K, OBS)).T
    rhs[:, K:] = d_rows.astype(BF16)
    for t in range(9):
        weighted[t * K : (t + 1) * K, :] = (perturb_t * effective[t : t + 1, :]).astype(BF16)
    right = rhs[...]
    for t in range(9):
        product = mm(weighted[t * K : (t + 1) * K, :], right)
        gram[t, :K, :] = product[:, :K]
        gram[t, K:, :] = jnp.broadcast_to(
            jnp.sum(product[:, K:] * eye, axis=0, keepdims=True), (GROWS - K, K)
        )

    def for_sides(pairs, act):
        for there, copy in pairs:

            @pl.when(there)
            def _(copy=copy):
                act(copy)

    gx_out = [
        (east, remote(gram.at[pl.ds(0, 3)], gram_x.at[0], send_gx.at[0], recv_gx.at[0], (gx + 1, gy))),
        (west, remote(gram.at[pl.ds(6, 3)], gram_x.at[1], send_gx.at[1], recv_gx.at[1], (gx - 1, gy))),
    ]
    gx_in = [(west, gx_out[0][1]), (east, gx_out[1][1])]
    for_sides(gx_out, lambda copy: copy.start())

    lines = 8

    def prepare(c, _):
        size = lines * TY
        rows = pl.ds(pl.multiple_of(c * size, size), size)
        members = field_v[rows, :]
        center = mm(members, mean)
        acc[rows, :] = center
        deviation = members.astype(F32) - center
        low, middle, top = by_tab[0], by_tab[1], by_tab[2]
        for n in range(lines):
            line = (c * lines + n) & (TX - 1)
            piece = deviation[n * TY : (n + 1) * TY]
            at = pl.ds(pl.multiple_of(c * size + n * TY, TY), TY)
            scaled[at, :K] = (piece * low).astype(BF16)
            scaled[at, K : 2 * K] = (piece * middle).astype(BF16)
            scaled[at, 2 * K :] = (piece * top).astype(BF16)
            u_side[at, :] = by_line(bx_tab, 1, line, piece).astype(BF16)
            s_own[at, :] = (piece * by_line(bx_tab, 1, line, middle)).astype(BF16)
        return 0

    steps = 2 * TX // lines
    lax.fori_loop(0, steps // 2, prepare, 0)

    for copy in ring:
        copy.wait_recv()
    sum_b[0] = jnp.sum(sum_a[...], axis=0)
    cross = [
        remote(sum_b.at[0], sum_b.at[k], send_b.at[k], recv_b.at[k], plane_peer(k))
        for k in range(1, planes)
    ]
    for copy in cross:
        copy.start()

    for_sides(gx_in, lambda copy: copy.wait_recv())
    half[0] = gram[3] + gram_x[0, 0] + gram_x[1, 0]
    half[1] = gram[5] + gram_x[0, 2] + gram_x[1, 2]
    gy_out = [
        (north, remote(half.at[0], gram_y.at[0], send_gy.at[0], recv_gy.at[0], (gx, gy + 1))),
        (south, remote(half.at[1], gram_y.at[1], send_gy.at[1], recv_gy.at[1], (gx, gy - 1))),
    ]
    gy_in = [(south, gy_out[0][1]), (north, gy_out[1][1])]
    for_sides(gy_out, lambda copy: copy.start())

    lax.fori_loop(steps // 2, steps, prepare, 0)

    for_sides(gy_in, lambda copy: copy.wait_recv())
    total = gram[4] + gram_x[0, 1] + gram_x[1, 1] + gram_y[0] + gram_y[1]
    projected = jnp.broadcast_to(total[K : K + 1], (K, K)).T
    total = total[:K]

    for copy in cross:
        copy.wait_recv()
    sums = jnp.sum(sum_b[...], axis=0)
    numerator = jnp.sum(jnp.where(lanes < K // 2, sums, 0.0), axis=1, keepdims=True)
    denominator = jnp.sum(jnp.where(lanes < K // 2, 0.0, sums), axis=1, keepdims=True)
    inflation = numerator / denominator

    system = eye / inflation + total / (K - 1)
    frob = jnp.sqrt(jnp.sum(jnp.sum(system * system, axis=0, keepdims=True), axis=1, keepdims=True))
    root = system / frob
    inv_root = None
    for sweep in range(NSTEPS):
        joint = root if sweep == 0 else high(inv_root, root)
        correction = 1.5 * eye - 0.5 * joint
        if sweep < NSTEPS - 1:
            root = high(root, correction)
        inv_root = correction if sweep == 0 else high(correction, inv_root)
    shift = high(inv_root, high(inv_root, projected)) / (frob * (K - 1))
    w_all[1, 1] = (inv_root / jnp.sqrt(frob) + shift).astype(BF16)

    mine = w_all.at[1, 1]
    wy_out = [
        (north, remote(mine, w_all.at[1, 0], send_wy.at[0], recv_wy.at[0], (gx, gy + 1))),
        (south, remote(mine, w_all.at[1, 2], send_wy.at[1], recv_wy.at[1], (gx, gy - 1))),
    ]
    wy_in = [(south, wy_out[0][1]), (north, wy_out[1][1])]
    wx_out = [
        (east, remote(mine, w_all.at[0, 1], send_wx.at[0], recv_wx.at[0], (gx + 1, gy))),
        (west, remote(mine, w_all.at[2, 1], send_wx.at[1], recv_wx.at[1], (gx - 1, gy))),
    ]
    wx_in = [(west, wx_out[0][1]), (east, wx_out[1][1])]
    for_sides(wy_out, lambda copy: copy.start())
    for_sides(wx_out, lambda copy: copy.start())

    size = 16 * TY

    def own(c, _):
        rows = pl.ds(pl.multiple_of(c * size, size), size)
        acc[rows, :] = acc[rows, :] + mm(s_own[rows, :], w_all[1, 1])
        return 0

    lax.fori_loop(0, CELLS // size, own, 0, unroll=2)

    for_sides(wy_in, lambda copy: copy.wait_recv())
    wc_out = []
    wc_in = []
    for n, (from_y, q) in enumerate(((south, 0), (north, 2))):
        to_e = remote(w_all.at[1, q], w_all.at[0, q], send_wc.at[0, n], recv_wc.at[0, n], (gx + 1, gy))
        to_w = remote(w_all.at[1, q], w_all.at[2, q], send_wc.at[1, n], recv_wc.at[1, n], (gx - 1, gy))
        wc_out += [(jnp.logical_and(from_y, east), to_e), (jnp.logical_and(from_y, west), to_w)]
        wc_in += [(jnp.logical_and(from_y, west), to_e), (jnp.logical_and(from_y, east), to_w)]
    for_sides(wc_out, lambda copy: copy.start())

    def along_gy(c, _):
        rows = pl.ds(pl.multiple_of(c * size, size), size)
        product = mm(u_side[rows, :], jnp.concatenate([w_all[1, 0], w_all[1, 2]], axis=1))
        low, top = by_tab[0], by_tab[2]
        for n in range(size // TY):
            cut = slice(n * TY, (n + 1) * TY)
            at = pl.ds(pl.multiple_of(c * size + n * TY, TY), TY)
            acc[at, :] = acc[at, :] + (low * product[cut, :K] + top * product[cut, K:])
        return 0

    lax.fori_loop(0, CELLS // size, along_gy, 0, unroll=2)

    for_sides(wx_in, lambda copy: copy.wait_recv())
    for_sides(wc_in, lambda copy: copy.wait_recv())
    for q in range(3):
        sides_w[q * K : (q + 1) * K, :K] = w_all[0, q]
        sides_w[q * K : (q + 1) * K, K:] = w_all[2, q]

    for copy in ring + cross:
        copy.wait_send()
    for_sides(gx_out + gy_out + wy_out + wx_out + wc_out, lambda copy: copy.wait_send())


def local(n_gx, n_gy, background, cell_index, obs_value, obs_inverse, obs_count, taper):
    levels, tile_x, tile_y, members = background.shape
    field = background.reshape(-1, members)
    cells = cell_index.reshape(1, OBS)
    smem = pl.BlockSpec(memory_space=pltpu.SMEM)
    vmem = pl.BlockSpec(memory_space=pltpu.VMEM)
    dma = pltpu.SemaphoreType.DMA
    planes = n_gx // BLOCK * n_gy
    parts = pl.pallas_call(
        functools.partial(kernel, n_gx, n_gy),
        out_shape=(
            pltpu.VMEM((CELLS, K), F32),
            pltpu.VMEM((CELLS, 3 * K), BF16),
            pltpu.VMEM((3 * K, 2 * K), BF16),
            pltpu.VMEM((3, TX, 8, K), F32),
        ),
        in_specs=[pl.BlockSpec(memory_space=pltpu.HBM), smem, vmem, vmem, vmem, smem, smem],
        out_specs=(vmem, vmem, vmem, vmem),
        scratch_shapes=[
            pltpu.VMEM((CELLS, K), BF16),
            pltpu.VMEM((CELLS, K), BF16),
            pltpu.VMEM((CELLS, K), BF16),
            pltpu.VMEM((3, TY, K), F32),
            pltpu.VMEM((OBS, K), F32),
            pltpu.VMEM((9 * K, OBS), BF16),
            pltpu.VMEM((OBS, 2 * K), BF16),
            pltpu.VMEM((9, GROWS, K), F32),
            pltpu.VMEM((2, 3, GROWS, K), F32),
            pltpu.VMEM((2, GROWS, K), F32),
            pltpu.VMEM((2, GROWS, K), F32),
            pltpu.VMEM((BLOCK, 1, K), F32),
            pltpu.VMEM((planes, 1, K), F32),
            pltpu.VMEM((3, 3, K, K), BF16),
            dma((LOADS,)),
            dma((BLOCK,)),
            dma((BLOCK,)),
            dma((planes,)),
            dma((planes,)),
            dma((2,)),
            dma((2,)),
            dma((2,)),
            dma((2,)),
            dma((2,)),
            dma((2,)),
            dma((2,)),
            dma((2,)),
            dma((2, 2)),
            dma((2, 2)),
        ],
        compiler_params=pltpu.CompilerParams(
            collective_id=0, has_side_effects=True, vmem_limit_bytes=20 * 1024 * 1024
        ),
    )(
        field,
        cells,
        cells,
        obs_value.reshape(1, OBS),
        obs_inverse.reshape(1, OBS),
        obs_count.reshape(1, 1),
        taper.reshape(1, BINS),
    )
    result = pl.pallas_call(
        last_pass,
        out_shape=jax.ShapeDtypeStruct((CELLS, K), BF16),
        in_specs=[vmem] * 4,
        out_specs=pl.BlockSpec(memory_space=pltpu.HBM),
        scratch_shapes=[pltpu.VMEM((CELLS, K), BF16), dma((CELLS // (16 * TY),))],
        compiler_params=pltpu.CompilerParams(vmem_limit_bytes=16 * 1024 * 1024),
    )(*parts)
    return result.reshape(levels, tile_x, tile_y, members)


def solution(mesh):
    in_specs = (
        P(None, "gx", "gy", None),
        P("gx", "gy", None),
        P("gx", "gy", None),
        P("gx", "gy", None),
        P("gx", "gy"),
        P(),
    )
    out_specs = P(None, "gx", "gy", None)
    step = functools.partial(local, mesh.shape["gx"], mesh.shape["gy"])
    return jax.shard_map(step, mesh=mesh, in_specs=in_specs, out_specs=out_specs, check_vma=False)
```

```python
import functools

import jax
import jax.numpy as jnp
from jax import lax
from jax.experimental import pallas as pl
from jax.experimental.pallas import tpu as pltpu
from jax.sharding import PartitionSpec as P

NSTEPS = 6
MESH = pl.DeviceIdType.MESH
F32 = jnp.float32
BF16 = jnp.bfloat16

K = 128
OBS = 512
TX = 64
TY = 128
BINS = 64
LIMIT = 9 * (TX * TX + TY * TY)
CELLS = 2 * TX * TY
LOADS = 8
GROWS = K + 8
BLOCK = 16


def nt(a, b):
    return lax.dot_general(a, b, (((1,), (1,)), ((), ())), preferred_element_type=F32)


def mm(a, b):
    return jnp.dot(a, b, preferred_element_type=F32)


def product3(a, b):
    a_top, b_top = a.astype(BF16), b.astype(BF16)
    a_rest = (a - a_top.astype(F32)).astype(BF16)
    b_rest = (b - b_top.astype(F32)).astype(BF16)
    return mm(
        jnp.concatenate([a_top, a_rest, a_top], axis=1),
        jnp.concatenate([b_top, b_top, b_rest], axis=0),
    )


def beta(position, has_low, has_high):
    low = 0.5 * ((1.0 - position) * (1.0 - position))
    middle = 0.5 + position - position * position
    top = 0.5 * (position * position)
    middle = middle + (1.0 - has_low) * low + (1.0 - has_high) * top
    return low * has_low, middle, top * has_high


def by_line(table, p, line, x):
    return (x.reshape(TY // 8, 8, K) * table[p, line][None]).reshape(TY, K)


def last_pass(acc, scaled, sides_w, bx_tab, out, result, out_sem):
    size = 16 * TY
    copies = [
        pltpu.make_async_copy(
            result.at[pl.ds(c * size, size), :], out.at[pl.ds(c * size, size), :], out_sem.at[c]
        )
        for c in range(CELLS // size)
    ]

    for c in range(CELLS // size):
        product = mm(scaled[c * size : (c + 1) * size, :], sides_w[...])
        for n in range(size // TY):
            line = (c * (size // TY) + n) % TX
            cut = slice(n * TY, (n + 1) * TY)
            at = slice(c * size + n * TY, c * size + (n + 1) * TY)
            result[at, :] = (
                acc[at, :]
                + by_line(bx_tab, 0, line, product[cut, :K])
                + by_line(bx_tab, 2, line, product[cut, K:])
            ).astype(BF16)
        copies[c].start()
    for copy in copies:
        copy.wait()


def kernel(
    n_gx,
    n_gy,
    field,
    cell_h,
    value_h,
    inverse_h,
    count,
    taper_h,
    acc,
    scaled,
    sides_w,
    bx_tab,
    field_v,
    s_own,
    u_side,
    by_tab,
    cell_s,
    cell_v,
    value,
    inverse,
    taper,
    picked,
    weighted,
    rhs,
    gram,
    gram_x,
    half,
    gram_y,
    sum_a,
    sum_b,
    w_all,
    load_sem,
    small_sem,
    send_a,
    recv_a,
    send_b,
    recv_b,
    send_gx,
    recv_gx,
    send_gy,
    recv_gy,
    send_wy,
    recv_wy,
    send_wx,
    recv_wx,
    send_wc,
    recv_wc,
):
    gx = lax.axis_index("gx")
    gy = lax.axis_index("gy")
    span = CELLS // LOADS
    loads = [
        pltpu.make_async_copy(
            field.at[pl.ds(k * span, span), :], field_v.at[pl.ds(k * span, span), :], load_sem.at[k]
        )
        for k in range(LOADS)
    ]
    small = [
        pltpu.make_async_copy(source, target, small_sem.at[k])
        for k, (source, target) in enumerate(
            (
                (cell_h, cell_v),
                (taper_h, taper),
                (inverse_h, inverse),
                (value_h, value),
                (cell_h, cell_s),
            )
        )
    ]
    for copy in small + loads:
        copy.start()

    gram_x[...] = jnp.zeros_like(gram_x)
    gram_y[...] = jnp.zeros_like(gram_y)
    w_all[...] = jnp.zeros_like(w_all)

    block = lax.div(gx, BLOCK)
    lane = lax.rem(gx, BLOCK)
    plane = block * n_gy + gy
    planes = n_gx // BLOCK * n_gy

    def ring_peer(k):
        return (block * BLOCK + lax.rem(lane + k, BLOCK), gy)

    def plane_peer(k):
        other = lax.rem(plane + k, planes)
        return (lax.div(other, n_gy) * BLOCK + lane, lax.rem(other, n_gy))

    west, east = gx > 0, gx < n_gx - 1
    south, north = gy > 0, gy < n_gy - 1
    sides = [
        (west, (gx - 1, gy)),
        (east, (gx + 1, gy)),
        (south, (gx, gy - 1)),
        (north, (gx, gy + 1)),
    ]

    barrier = pltpu.get_barrier_semaphore()
    for k in range(1, BLOCK):
        pl.semaphore_signal(barrier, inc=1, device_id=ring_peer(k), device_id_type=MESH)
    for k in range(1, planes):
        pl.semaphore_signal(barrier, inc=1, device_id=plane_peer(k), device_id_type=MESH)
    for there, peer in sides:

        @pl.when(there)
        def _(peer=peer):
            pl.semaphore_signal(barrier, inc=1, device_id=peer, device_id_type=MESH)

    has_s, has_n = south.astype(F32), north.astype(F32)
    has_w, has_e = west.astype(F32), east.astype(F32)
    v_pos = (lax.broadcasted_iota(jnp.int32, (TY, K), 0).astype(F32) + 0.5) / TY
    for q, part in enumerate(beta(v_pos, has_s, has_n)):
        by_tab[q] = part

    u_pos = (lax.broadcasted_iota(jnp.int32, (TX, 8, K), 0).astype(F32) + 0.5) / TX
    for p, part in enumerate(beta(u_pos, has_w, has_e)):
        bx_tab[p] = part

    for copy in small:
        copy.wait()

    cells = cell_v[...]
    col = lax.shift_right_logical(cells & (TX * TY - 1), 7)
    row = cells & (TY - 1)
    slot = lax.broadcasted_iota(jnp.int32, (1, OBS), 1)
    live = (slot < count[0, 0]).astype(F32)
    weight = (inverse[...] * live).astype(BF16).astype(F32)
    which = lax.broadcasted_iota(jnp.int32, (BLOCK, OBS), 0)
    third = lax.shift_right_logical(which * 11, 5)
    dx = 2 * ((third - 1) * TX + col) - (TX - 1)
    dy = 2 * ((which - third * 3 - 1) * TY + row) - (TY - 1)
    distance = (dx * dx + dy * dy) * BINS
    factor = jnp.zeros((BLOCK, OBS), F32)
    for n in range(BINS):
        factor = jnp.where(distance >= n * LIMIT, taper[0, n].astype(F32), factor)
    effective = weight * (factor / 1024.0)

    for k in range(LOADS):
        loads[k].wait()

        def widen(i, _, k=k):
            rows = pl.ds(pl.multiple_of(k * span + i * 256, 256), 256)
            acc[rows, :] = field_v[rows, :].astype(F32)
            return 0

        lax.fori_loop(0, span // 256, widen, 0, unroll=True)

    def pick(i, _):
        for k in range(16):
            s = i * 16 + k
            picked[pl.ds(s, 1), :] = acc[pl.ds(cell_s[0, s], 1), :]
        return 0

    lax.fori_loop(0, OBS // 16, pick, 0)

    mean = jnp.full((K, K), 1.0 / K, BF16)
    cols = lax.broadcasted_iota(jnp.int32, (K, K), 1)
    rows_ = lax.broadcasted_iota(jnp.int32, (K, K), 0)
    eye = (cols == rows_).astype(F32)
    chosen = picked[...]
    chosen_b = chosen.astype(BF16)
    center_b = mm(chosen_b, mean)
    center_r = nt(mean[:16], chosen_b)[:1]
    perturb = (chosen - center_b).astype(BF16)
    perturb_t = nt(eye.astype(BF16), perturb)
    innovation = (value[...] - center_r).astype(BF16).astype(F32)
    spread = jnp.sum(perturb_t * perturb_t, axis=0, keepdims=True) / (K - 1)
    num = weight * innovation * innovation
    den = weight * spread + live
    num = num[:, :K] + num[:, K : 2 * K] + num[:, 2 * K : 3 * K] + num[:, 3 * K :]
    den = den[:, :K] + den[:, K : 2 * K] + den[:, 2 * K : 3 * K] + den[:, 3 * K :]
    num = num + pltpu.roll(num, K // 2, 1)
    den = den + pltpu.roll(den, K // 2, 1)
    lanes = lax.broadcasted_iota(jnp.int32, (1, K), 1)
    sum_a[0] = jnp.where(lanes < K // 2, num, den)

    pl.semaphore_wait(
        barrier,
        BLOCK - 1
        + planes - 1
        + west.astype(jnp.int32)
        + east.astype(jnp.int32)
        + south.astype(jnp.int32)
        + north.astype(jnp.int32),
    )

    def remote(src, dst, send, recv, peer):
        return pltpu.make_async_remote_copy(
            src_ref=src, dst_ref=dst, send_sem=send, recv_sem=recv, device_id=peer, device_id_type=MESH
        )

    ring = [
        remote(sum_a.at[0], sum_a.at[k], send_a.at[k], recv_a.at[k], ring_peer(k))
        for k in range(1, BLOCK)
    ]
    for copy in ring:
        copy.start()

    rhs[:, :K] = perturb
    d_rows = jnp.broadcast_to(innovation, (K, OBS)).T
    rhs[:, K:] = d_rows.astype(BF16)
    for t in range(9):
        weighted[t * K : (t + 1) * K, :] = (perturb_t * effective[t : t + 1, :]).astype(BF16)
    right = rhs[...]
    for t in range(9):
        product = mm(weighted[t * K : (t + 1) * K, :], right)
        gram[t, :K, :] = product[:, :K]
        gram[t, K:, :] = jnp.broadcast_to(
            jnp.sum(product[:, K:] * eye, axis=0, keepdims=True), (GROWS - K, K)
        )

    def for_sides(pairs, act):
        for there, copy in pairs:

            @pl.when(there)
            def _(copy=copy):
                act(copy)

    gx_out = [
        (east, remote(gram.at[pl.ds(0, 3)], gram_x.at[0], send_gx.at[0], recv_gx.at[0], (gx + 1, gy))),
        (west, remote(gram.at[pl.ds(6, 3)], gram_x.at[1], send_gx.at[1], recv_gx.at[1], (gx - 1, gy))),
    ]
    gx_in = [(west, gx_out[0][1]), (east, gx_out[1][1])]
    for_sides(gx_out, lambda copy: copy.start())

    lines = 8

    def prepare(c, _):
        size = lines * TY
        rows = pl.ds(pl.multiple_of(c * size, size), size)
        members = field_v[rows, :]
        center = mm(members, mean)
        acc[rows, :] = center
        deviation = members.astype(F32) - center
        low, middle, top = by_tab[0], by_tab[1], by_tab[2]
        for n in range(lines):
            line = (c * lines + n) & (TX - 1)
            piece = deviation[n * TY : (n + 1) * TY]
            at = pl.ds(pl.multiple_of(c * size + n * TY, TY), TY)
            scaled[at, :K] = (piece * low).astype(BF16)
            scaled[at, K : 2 * K] = (piece * middle).astype(BF16)
            scaled[at, 2 * K :] = (piece * top).astype(BF16)
            u_side[at, :] = by_line(bx_tab, 1, line, piece).astype(BF16)
            s_own[at, :] = (piece * by_line(bx_tab, 1, line, middle)).astype(BF16)
        return 0

    steps = 2 * TX // lines
    lax.fori_loop(0, steps // 2, prepare, 0, unroll=2)

    for copy in ring:
        copy.wait_recv()
    sum_b[0] = jnp.sum(sum_a[...], axis=0)
    cross = [
        remote(sum_b.at[0], sum_b.at[k], send_b.at[k], recv_b.at[k], plane_peer(k))
        for k in range(1, planes)
    ]
    for copy in cross:
        copy.start()

    for_sides(gx_in, lambda copy: copy.wait_recv())
    half[0] = gram[3] + gram_x[0, 0] + gram_x[1, 0]
    half[1] = gram[5] + gram_x[0, 2] + gram_x[1, 2]
    gy_out = [
        (north, remote(half.at[0], gram_y.at[0], send_gy.at[0], recv_gy.at[0], (gx, gy + 1))),
        (south, remote(half.at[1], gram_y.at[1], send_gy.at[1], recv_gy.at[1], (gx, gy - 1))),
    ]
    gy_in = [(south, gy_out[0][1]), (north, gy_out[1][1])]
    for_sides(gy_out, lambda copy: copy.start())

    lax.fori_loop(steps // 2, steps, prepare, 0, unroll=2)

    for_sides(gy_in, lambda copy: copy.wait_recv())
    total = gram[4] + gram_x[0, 1] + gram_x[1, 1] + gram_y[0] + gram_y[1]
    projected = jnp.broadcast_to(total[K : K + 1], (K, K)).T
    total = total[:K]

    for copy in cross:
        copy.wait_recv()
    sums = jnp.sum(sum_b[...], axis=0)
    numerator = jnp.sum(jnp.where(lanes < K // 2, sums, 0.0), axis=1, keepdims=True)
    denominator = jnp.sum(jnp.where(lanes < K // 2, 0.0, sums), axis=1, keepdims=True)
    inflation = numerator / denominator

    system = eye / inflation + total / (K - 1)
    frob = jnp.sqrt(jnp.sum(jnp.sum(system * system, axis=0, keepdims=True), axis=1, keepdims=True))
    root = system / frob
    correction = 1.5 * eye - 0.5 * root
    root = product3(correction, root)
    inv_root = correction
    for sweep in range(1, NSTEPS - 1):
        correction = 1.5 * eye - 0.5 * product3(inv_root, root)
        both = product3(correction, jnp.concatenate([root, inv_root], axis=1))
        root, inv_root = both[:, :K], both[:, K:]
    both = product3(inv_root, jnp.concatenate([root, projected], axis=1))
    correction = 1.5 * eye - 0.5 * both[:, :K]
    both = product3(correction, jnp.concatenate([inv_root, both[:, K:]], axis=1))
    inv_root = both[:, :K]
    shift = product3(inv_root, both[:, K:]) / (frob * (K - 1))
    w_all[1, 1] = (inv_root / jnp.sqrt(frob) + shift).astype(BF16)

    mine = w_all.at[1, 1]
    wy_out = [
        (north, remote(mine, w_all.at[1, 0], send_wy.at[0], recv_wy.at[0], (gx, gy + 1))),
        (south, remote(mine, w_all.at[1, 2], send_wy.at[1], recv_wy.at[1], (gx, gy - 1))),
    ]
    wy_in = [(south, wy_out[0][1]), (north, wy_out[1][1])]
    wx_out = [
        (east, remote(mine, w_all.at[0, 1], send_wx.at[0], recv_wx.at[0], (gx + 1, gy))),
        (west, remote(mine, w_all.at[2, 1], send_wx.at[1], recv_wx.at[1], (gx - 1, gy))),
    ]
    wx_in = [(west, wx_out[0][1]), (east, wx_out[1][1])]
    for_sides(wy_out, lambda copy: copy.start())
    for_sides(wx_out, lambda copy: copy.start())

    size = 16 * TY

    def own(c, _):
        rows = pl.ds(pl.multiple_of(c * size, size), size)
        acc[rows, :] = acc[rows, :] + mm(s_own[rows, :], w_all[1, 1])
        return 0

    lax.fori_loop(0, CELLS // size, own, 0, unroll=2)

    for_sides(wy_in, lambda copy: copy.wait_recv())
    wc_out = []
    wc_in = []
    for n, (from_y, q) in enumerate(((south, 0), (north, 2))):
        to_e = remote(w_all.at[1, q], w_all.at[0, q], send_wc.at[0, n], recv_wc.at[0, n], (gx + 1, gy))
        to_w = remote(w_all.at[1, q], w_all.at[2, q], send_wc.at[1, n], recv_wc.at[1, n], (gx - 1, gy))
        wc_out += [(jnp.logical_and(from_y, east), to_e), (jnp.logical_and(from_y, west), to_w)]
        wc_in += [(jnp.logical_and(from_y, west), to_e), (jnp.logical_and(from_y, east), to_w)]
    for_sides(wc_out, lambda copy: copy.start())

    def along_gy(c, _):
        rows = pl.ds(pl.multiple_of(c * size, size), size)
        product = mm(u_side[rows, :], jnp.concatenate([w_all[1, 0], w_all[1, 2]], axis=1))
        low, top = by_tab[0], by_tab[2]
        for n in range(size // TY):
            cut = slice(n * TY, (n + 1) * TY)
            at = pl.ds(pl.multiple_of(c * size + n * TY, TY), TY)
            acc[at, :] = acc[at, :] + (low * product[cut, :K] + top * product[cut, K:])
        return 0

    lax.fori_loop(0, CELLS // size, along_gy, 0, unroll=2)

    for_sides(wx_in, lambda copy: copy.wait_recv())
    for_sides(wc_in, lambda copy: copy.wait_recv())
    for q in range(3):
        sides_w[q * K : (q + 1) * K, :K] = w_all[0, q]
        sides_w[q * K : (q + 1) * K, K:] = w_all[2, q]

    for copy in ring + cross:
        copy.wait_send()
    for_sides(gx_out + gy_out + wy_out + wx_out + wc_out, lambda copy: copy.wait_send())


def local(n_gx, n_gy, background, cell_index, obs_value, obs_inverse, obs_count, taper):
    levels, tile_x, tile_y, members = background.shape
    field = background.reshape(-1, members)
    cells = cell_index.reshape(1, OBS)
    vmem = pl.BlockSpec(memory_space=pltpu.VMEM)
    hbm = pl.BlockSpec(memory_space=pltpu.HBM)
    dma = pltpu.SemaphoreType.DMA
    planes = n_gx // BLOCK * n_gy
    pin = functools.partial(pltpu.with_memory_space_constraint, memory_space=pltpu.HBM)
    parts = pl.pallas_call(
        functools.partial(kernel, n_gx, n_gy),
        out_shape=(
            pltpu.VMEM((CELLS, K), F32),
            pltpu.VMEM((CELLS, 3 * K), BF16),
            pltpu.VMEM((3 * K, 2 * K), BF16),
            pltpu.VMEM((3, TX, 8, K), F32),
        ),
        in_specs=[hbm, hbm, hbm, hbm, pl.BlockSpec(memory_space=pltpu.SMEM), hbm],
        out_specs=(vmem, vmem, vmem, vmem),
        scratch_shapes=[
            pltpu.VMEM((CELLS, K), BF16),
            pltpu.VMEM((CELLS, K), BF16),
            pltpu.VMEM((CELLS, K), BF16),
            pltpu.VMEM((3, TY, K), F32),
            pltpu.SMEM((1, OBS), jnp.int32),
            pltpu.VMEM((1, OBS), jnp.int32),
            pltpu.VMEM((1, OBS), F32),
            pltpu.VMEM((1, OBS), F32),
            pltpu.SMEM((1, BINS), jnp.int32),
            pltpu.VMEM((OBS, K), F32),
            pltpu.VMEM((9 * K, OBS), BF16),
            pltpu.VMEM((OBS, 2 * K), BF16),
            pltpu.VMEM((9, GROWS, K), F32),
            pltpu.VMEM((2, 3, GROWS, K), F32),
            pltpu.VMEM((2, GROWS, K), F32),
            pltpu.VMEM((2, GROWS, K), F32),
            pltpu.VMEM((BLOCK, 1, K), F32),
            pltpu.VMEM((planes, 1, K), F32),
            pltpu.VMEM((3, 3, K, K), BF16),
            dma((LOADS,)),
            dma((5,)),
            dma((BLOCK,)),
            dma((BLOCK,)),
            dma((planes,)),
            dma((planes,)),
            dma((2,)),
            dma((2,)),
            dma((2,)),
            dma((2,)),
            dma((2,)),
            dma((2,)),
            dma((2,)),
            dma((2,)),
            dma((2, 2)),
            dma((2, 2)),
        ],
        compiler_params=pltpu.CompilerParams(
            collective_id=0, has_side_effects=True, vmem_limit_bytes=20 * 1024 * 1024
        ),
    )(
        pin(field),
        pin(cells),
        pin(obs_value.reshape(1, OBS)),
        pin(obs_inverse.reshape(1, OBS)),
        obs_count.reshape(1, 1),
        pin(taper.reshape(1, BINS)),
    )
    result = pl.pallas_call(
        last_pass,
        out_shape=jax.ShapeDtypeStruct((CELLS, K), BF16),
        in_specs=[vmem] * 4,
        out_specs=pl.BlockSpec(memory_space=pltpu.HBM),
        scratch_shapes=[pltpu.VMEM((CELLS, K), BF16), dma((CELLS // (16 * TY),))],
        compiler_params=pltpu.CompilerParams(vmem_limit_bytes=16 * 1024 * 1024),
    )(*parts)
    return result.reshape(levels, tile_x, tile_y, members)


def solution(mesh):
    in_specs = (
        P(None, "gx", "gy", None),
        P("gx", "gy", None),
        P("gx", "gy", None),
        P("gx", "gy", None),
        P("gx", "gy"),
        P(),
    )
    out_specs = P(None, "gx", "gy", None)
    step = functools.partial(local, mesh.shape["gx"], mesh.shape["gy"])
    return jax.shard_map(step, mesh=mesh, in_specs=in_specs, out_specs=out_specs, check_vma=False)
```

```python
import functools

import jax
import jax.numpy as jnp
from jax import lax
from jax.experimental import pallas as pl
from jax.experimental.pallas import tpu as pltpu
from jax.sharding import PartitionSpec as P

NSTEPS = 6
MESH = pl.DeviceIdType.MESH
F32 = jnp.float32
BF16 = jnp.bfloat16

K = 128
OBS = 512
TX = 64
TY = 128
BINS = 64
LIMIT = 9 * (TX * TX + TY * TY)
CELLS = 2 * TX * TY
LOADS = 8
GROWS = K + 8
BLOCK = 16


def nt(a, b):
    return lax.dot_general(a, b, (((1,), (1,)), ((), ())), preferred_element_type=F32)


def mm(a, b):
    return jnp.dot(a, b, preferred_element_type=F32)


def product3(a, b):
    a_top, b_top = a.astype(BF16), b.astype(BF16)
    a_rest = (a - a_top.astype(F32)).astype(BF16)
    b_rest = (b - b_top.astype(F32)).astype(BF16)
    return mm(
        jnp.concatenate([a_top, a_rest, a_top], axis=1),
        jnp.concatenate([b_top, b_top, b_rest], axis=0),
    )


def beta(position, has_low, has_high):
    low = 0.5 * ((1.0 - position) * (1.0 - position))
    middle = 0.5 + position - position * position
    top = 0.5 * (position * position)
    middle = middle + (1.0 - has_low) * low + (1.0 - has_high) * top
    return low * has_low, middle, top * has_high


def by_line(table, p, line, x):
    return (x.reshape(TY // 8, 8, K) * table[p, line][None]).reshape(TY, K)


def last_pass(acc, scaled, sides_w, bx_tab, out, result, out_sem):
    size = 8 * TY
    copies = [
        pltpu.make_async_copy(
            result.at[pl.ds(c * size, size), :], out.at[pl.ds(c * size, size), :], out_sem.at[c]
        )
        for c in range(CELLS // size)
    ]

    for c in range(CELLS // size):
        product = mm(scaled[c * size : (c + 1) * size, :], sides_w[...])
        for n in range(size // TY):
            line = (c * (size // TY) + n) % TX
            cut = slice(n * TY, (n + 1) * TY)
            at = slice(c * size + n * TY, c * size + (n + 1) * TY)
            result[at, :] = (
                acc[at, :]
                + by_line(bx_tab, 0, line, product[cut, :K])
                + by_line(bx_tab, 2, line, product[cut, K:])
            ).astype(BF16)
        copies[c].start()
    for copy in copies:
        copy.wait()


def kernel(
    n_gx,
    n_gy,
    field,
    cell_h,
    value_h,
    inverse_h,
    count,
    taper_h,
    acc,
    scaled,
    sides_w,
    bx_tab,
    field_v,
    s_own,
    u_side,
    by_tab,
    cell_s,
    cell_v,
    value,
    inverse,
    taper,
    picked,
    weighted,
    rhs,
    gram,
    gram_x,
    half,
    gram_y,
    sum_a,
    sum_b,
    w_all,
    load_sem,
    small_sem,
    send_a,
    recv_a,
    send_b,
    recv_b,
    send_gx,
    recv_gx,
    send_gy,
    recv_gy,
    send_wy,
    recv_wy,
    send_wx,
    recv_wx,
    send_wc,
    recv_wc,
):
    gx = lax.axis_index("gx")
    gy = lax.axis_index("gy")
    span = CELLS // LOADS
    loads = [
        pltpu.make_async_copy(
            field.at[pl.ds(k * span, span), :], field_v.at[pl.ds(k * span, span), :], load_sem.at[k]
        )
        for k in range(LOADS)
    ]
    small = [
        pltpu.make_async_copy(source, target, small_sem.at[k])
        for k, (source, target) in enumerate(
            (
                (cell_h, cell_v),
                (taper_h, taper),
                (inverse_h, inverse),
                (value_h, value),
                (cell_h, cell_s),
            )
        )
    ]
    for copy in small + loads:
        copy.start()

    gram_x[...] = jnp.zeros_like(gram_x)
    gram_y[...] = jnp.zeros_like(gram_y)
    w_all[...] = jnp.zeros_like(w_all)

    block = lax.div(gx, BLOCK)
    lane = lax.rem(gx, BLOCK)
    plane = block * n_gy + gy
    planes = n_gx // BLOCK * n_gy

    def ring_peer(k):
        return (block * BLOCK + lax.rem(lane + k, BLOCK), gy)

    def plane_peer(k):
        other = lax.rem(plane + k, planes)
        return (lax.div(other, n_gy) * BLOCK + lane, lax.rem(other, n_gy))

    west, east = gx > 0, gx < n_gx - 1
    south, north = gy > 0, gy < n_gy - 1
    sides = [
        (west, (gx - 1, gy)),
        (east, (gx + 1, gy)),
        (south, (gx, gy - 1)),
        (north, (gx, gy + 1)),
    ]

    barrier = pltpu.get_barrier_semaphore()
    for k in range(1, BLOCK):
        pl.semaphore_signal(barrier, inc=1, device_id=ring_peer(k), device_id_type=MESH)
    for k in range(1, planes):
        pl.semaphore_signal(barrier, inc=1, device_id=plane_peer(k), device_id_type=MESH)
    for there, peer in sides:

        @pl.when(there)
        def _(peer=peer):
            pl.semaphore_signal(barrier, inc=1, device_id=peer, device_id_type=MESH)

    has_s, has_n = south.astype(F32), north.astype(F32)
    has_w, has_e = west.astype(F32), east.astype(F32)
    v_pos = (lax.broadcasted_iota(jnp.int32, (TY, K), 0).astype(F32) + 0.5) / TY
    for q, part in enumerate(beta(v_pos, has_s, has_n)):
        by_tab[q] = part

    u_pos = (lax.broadcasted_iota(jnp.int32, (TX, 8, K), 0).astype(F32) + 0.5) / TX
    for p, part in enumerate(beta(u_pos, has_w, has_e)):
        bx_tab[p] = part

    for copy in small:
        copy.wait()

    cells = cell_v[...]
    col = lax.shift_right_logical(cells & (TX * TY - 1), 7)
    row = cells & (TY - 1)
    slot = lax.broadcasted_iota(jnp.int32, (1, OBS), 1)
    live = (slot < count[0, 0]).astype(F32)
    weight = (inverse[...] * live).astype(BF16).astype(F32)
    which = lax.broadcasted_iota(jnp.int32, (BLOCK, OBS), 0)
    third = lax.shift_right_logical(which * 11, 5)
    dx = 2 * ((third - 1) * TX + col) - (TX - 1)
    dy = 2 * ((which - third * 3 - 1) * TY + row) - (TY - 1)
    distance = (dx * dx + dy * dy) * BINS
    factor = jnp.zeros((BLOCK, OBS), F32)
    for n in range(BINS):
        factor = jnp.where(distance >= n * LIMIT, taper[0, n].astype(F32), factor)
    effective = weight * (factor / 1024.0)

    for k in range(LOADS):
        loads[k].wait()

        def widen(i, _, k=k):
            rows = pl.ds(pl.multiple_of(k * span + i * 256, 256), 256)
            acc[rows, :] = field_v[rows, :].astype(F32)
            return 0

        lax.fori_loop(0, span // 256, widen, 0, unroll=True)

    def pick(i, _):
        for k in range(16):
            s = i * 16 + k
            picked[pl.ds(s, 1), :] = acc[pl.ds(cell_s[0, s], 1), :]
        return 0

    lax.fori_loop(0, OBS // 16, pick, 0)

    mean = jnp.full((K, K), 1.0 / K, BF16)
    cols = lax.broadcasted_iota(jnp.int32, (K, K), 1)
    rows_ = lax.broadcasted_iota(jnp.int32, (K, K), 0)
    eye = (cols == rows_).astype(F32)
    chosen = picked[...]
    chosen_b = chosen.astype(BF16)
    center_b = mm(chosen_b, mean)
    center_r = nt(mean[:16], chosen_b)[:1]
    perturb = (chosen - center_b).astype(BF16)
    perturb_t = nt(eye.astype(BF16), perturb)
    innovation = (value[...] - center_r).astype(BF16).astype(F32)
    spread = jnp.sum(perturb_t * perturb_t, axis=0, keepdims=True) / (K - 1)
    num = weight * innovation * innovation
    den = weight * spread + live
    num = num[:, :K] + num[:, K : 2 * K] + num[:, 2 * K : 3 * K] + num[:, 3 * K :]
    den = den[:, :K] + den[:, K : 2 * K] + den[:, 2 * K : 3 * K] + den[:, 3 * K :]
    num = num + pltpu.roll(num, K // 2, 1)
    den = den + pltpu.roll(den, K // 2, 1)
    lanes = lax.broadcasted_iota(jnp.int32, (1, K), 1)
    sum_a[0] = jnp.where(lanes < K // 2, num, den)

    pl.semaphore_wait(
        barrier,
        BLOCK - 1
        + planes - 1
        + west.astype(jnp.int32)
        + east.astype(jnp.int32)
        + south.astype(jnp.int32)
        + north.astype(jnp.int32),
    )

    def remote(src, dst, send, recv, peer):
        return pltpu.make_async_remote_copy(
            src_ref=src, dst_ref=dst, send_sem=send, recv_sem=recv, device_id=peer, device_id_type=MESH
        )

    ring = [
        remote(sum_a.at[0], sum_a.at[k], send_a.at[k], recv_a.at[k], ring_peer(k))
        for k in range(1, BLOCK)
    ]
    for copy in ring:
        copy.start()

    rhs[:, :K] = perturb
    d_rows = jnp.broadcast_to(innovation, (K, OBS)).T
    rhs[:, K:] = d_rows.astype(BF16)
    for t in range(9):
        weighted[t * K : (t + 1) * K, :] = (perturb_t * effective[t : t + 1, :]).astype(BF16)
    right = rhs[...]
    for t in range(9):
        product = mm(weighted[t * K : (t + 1) * K, :], right)
        gram[t, :K, :] = product[:, :K]
        gram[t, K:, :] = jnp.broadcast_to(
            jnp.sum(product[:, K:] * eye, axis=0, keepdims=True), (GROWS - K, K)
        )

    def for_sides(pairs, act):
        for there, copy in pairs:

            @pl.when(there)
            def _(copy=copy):
                act(copy)

    gx_out = [
        (east, remote(gram.at[pl.ds(0, 3)], gram_x.at[0], send_gx.at[0], recv_gx.at[0], (gx + 1, gy))),
        (west, remote(gram.at[pl.ds(6, 3)], gram_x.at[1], send_gx.at[1], recv_gx.at[1], (gx - 1, gy))),
    ]
    gx_in = [(west, gx_out[0][1]), (east, gx_out[1][1])]
    for_sides(gx_out, lambda copy: copy.start())

    lines = 8

    def prepare(c, _):
        size = lines * TY
        rows = pl.ds(pl.multiple_of(c * size, size), size)
        members = field_v[rows, :]
        center = mm(members, mean)
        acc[rows, :] = center
        deviation = members.astype(F32) - center
        low, middle, top = by_tab[0], by_tab[1], by_tab[2]
        for n in range(lines):
            line = (c * lines + n) & (TX - 1)
            piece = deviation[n * TY : (n + 1) * TY]
            at = pl.ds(pl.multiple_of(c * size + n * TY, TY), TY)
            scaled[at, :K] = (piece * low).astype(BF16)
            scaled[at, K : 2 * K] = (piece * middle).astype(BF16)
            scaled[at, 2 * K :] = (piece * top).astype(BF16)
            s_own[at, :] = (piece * by_line(bx_tab, 1, line, middle)).astype(BF16)
            u_side[at, :] = by_line(bx_tab, 1, line, piece).astype(BF16)
        return 0

    steps = 2 * TX // lines
    lax.fori_loop(0, steps // 2, prepare, 0, unroll=True)

    for copy in ring:
        copy.wait_recv()
    sum_b[0] = jnp.sum(sum_a[...], axis=0)
    cross = [
        remote(sum_b.at[0], sum_b.at[k], send_b.at[k], recv_b.at[k], plane_peer(k))
        for k in range(1, planes)
    ]
    for copy in cross:
        copy.start()

    for_sides(gx_in, lambda copy: copy.wait_recv())
    half[0] = gram[3] + gram_x[0, 0] + gram_x[1, 0]
    half[1] = gram[5] + gram_x[0, 2] + gram_x[1, 2]
    gy_out = [
        (north, remote(half.at[0], gram_y.at[0], send_gy.at[0], recv_gy.at[0], (gx, gy + 1))),
        (south, remote(half.at[1], gram_y.at[1], send_gy.at[1], recv_gy.at[1], (gx, gy - 1))),
    ]
    gy_in = [(south, gy_out[0][1]), (north, gy_out[1][1])]
    for_sides(gy_out, lambda copy: copy.start())

    lax.fori_loop(steps // 2, steps, prepare, 0, unroll=True)

    for_sides(gy_in, lambda copy: copy.wait_recv())
    total = gram[4] + gram_x[0, 1] + gram_x[1, 1] + gram_y[0] + gram_y[1]
    projected = jnp.broadcast_to(total[K : K + 1], (K, K)).T
    total = total[:K]

    for copy in cross:
        copy.wait_recv()
    sums = jnp.sum(sum_b[...], axis=0)
    numerator = jnp.sum(jnp.where(lanes < K // 2, sums, 0.0), axis=1, keepdims=True)
    denominator = jnp.sum(jnp.where(lanes < K // 2, 0.0, sums), axis=1, keepdims=True)
    inflation = numerator / denominator

    system = eye / inflation + total / (K - 1)
    frob = jnp.sqrt(jnp.sum(jnp.sum(system * system, axis=0, keepdims=True), axis=1, keepdims=True))
    root = system / frob
    correction = 1.5 * eye - 0.5 * root
    root = product3(correction, root)
    inv_root = correction
    for sweep in range(1, NSTEPS - 1):
        correction = 1.5 * eye - 0.5 * product3(inv_root, root)
        both = product3(correction, jnp.concatenate([root, inv_root], axis=1))
        root, inv_root = both[:, :K], both[:, K:]
    both = product3(inv_root, jnp.concatenate([root, projected], axis=1))
    correction = 1.5 * eye - 0.5 * both[:, :K]
    both = product3(correction, jnp.concatenate([inv_root, both[:, K:]], axis=1))
    inv_root = both[:, :K]
    shift = product3(inv_root, both[:, K:]) / (frob * (K - 1))
    w_all[1, 1] = (inv_root / jnp.sqrt(frob) + shift).astype(BF16)

    mine = w_all.at[1, 1]
    wy_out = [
        (north, remote(mine, w_all.at[1, 0], send_wy.at[0], recv_wy.at[0], (gx, gy + 1))),
        (south, remote(mine, w_all.at[1, 2], send_wy.at[1], recv_wy.at[1], (gx, gy - 1))),
    ]
    wy_in = [(south, wy_out[0][1]), (north, wy_out[1][1])]
    wx_out = [
        (east, remote(mine, w_all.at[0, 1], send_wx.at[0], recv_wx.at[0], (gx + 1, gy))),
        (west, remote(mine, w_all.at[2, 1], send_wx.at[1], recv_wx.at[1], (gx - 1, gy))),
    ]
    wx_in = [(west, wx_out[0][1]), (east, wx_out[1][1])]
    for_sides(wy_out, lambda copy: copy.start())
    for_sides(wx_out, lambda copy: copy.start())

    size = 16 * TY

    def own(c, _):
        rows = pl.ds(pl.multiple_of(c * size, size), size)
        acc[rows, :] = acc[rows, :] + mm(s_own[rows, :], w_all[1, 1])
        return 0

    lax.fori_loop(0, CELLS // size, own, 0, unroll=True)

    for_sides(wy_in, lambda copy: copy.wait_recv())
    wc_out = []
    wc_in = []
    for n, (from_y, q) in enumerate(((south, 0), (north, 2))):
        to_e = remote(w_all.at[1, q], w_all.at[0, q], send_wc.at[0, n], recv_wc.at[0, n], (gx + 1, gy))
        to_w = remote(w_all.at[1, q], w_all.at[2, q], send_wc.at[1, n], recv_wc.at[1, n], (gx - 1, gy))
        wc_out += [(jnp.logical_and(from_y, east), to_e), (jnp.logical_and(from_y, west), to_w)]
        wc_in += [(jnp.logical_and(from_y, west), to_e), (jnp.logical_and(from_y, east), to_w)]
    for_sides(wc_out, lambda copy: copy.start())

    def along_gy(c, _):
        rows = pl.ds(pl.multiple_of(c * size, size), size)
        product = mm(u_side[rows, :], jnp.concatenate([w_all[1, 0], w_all[1, 2]], axis=1))
        low, top = by_tab[0], by_tab[2]
        for n in range(size // TY):
            cut = slice(n * TY, (n + 1) * TY)
            at = pl.ds(pl.multiple_of(c * size + n * TY, TY), TY)
            acc[at, :] = acc[at, :] + (low * product[cut, :K] + top * product[cut, K:])
        return 0

    lax.fori_loop(0, CELLS // size, along_gy, 0, unroll=True)

    for_sides(wx_in, lambda copy: copy.wait_recv())
    for_sides(wc_in, lambda copy: copy.wait_recv())
    for q in range(3):
        sides_w[q * K : (q + 1) * K, :K] = w_all[0, q]
        sides_w[q * K : (q + 1) * K, K:] = w_all[2, q]

    for copy in ring + cross:
        copy.wait_send()
    for_sides(gx_out + gy_out + wy_out + wx_out + wc_out, lambda copy: copy.wait_send())


def local(n_gx, n_gy, background, cell_index, obs_value, obs_inverse, obs_count, taper):
    levels, tile_x, tile_y, members = background.shape
    field = background.reshape(-1, members)
    cells = cell_index.reshape(1, OBS)
    vmem = pl.BlockSpec(memory_space=pltpu.VMEM)
    hbm = pl.BlockSpec(memory_space=pltpu.HBM)
    dma = pltpu.SemaphoreType.DMA
    planes = n_gx // BLOCK * n_gy
    pin = functools.partial(pltpu.with_memory_space_constraint, memory_space=pltpu.HBM)
    parts = pl.pallas_call(
        functools.partial(kernel, n_gx, n_gy),
        out_shape=(
            pltpu.VMEM((CELLS, K), F32),
            pltpu.VMEM((CELLS, 3 * K), BF16),
            pltpu.VMEM((3 * K, 2 * K), BF16),
            pltpu.VMEM((3, TX, 8, K), F32),
        ),
        in_specs=[hbm, hbm, hbm, hbm, pl.BlockSpec(memory_space=pltpu.SMEM), hbm],
        out_specs=(vmem, vmem, vmem, vmem),
        scratch_shapes=[
            pltpu.VMEM((CELLS, K), BF16),
            pltpu.VMEM((CELLS, K), BF16),
            pltpu.VMEM((CELLS, K), BF16),
            pltpu.VMEM((3, TY, K), F32),
            pltpu.SMEM((1, OBS), jnp.int32),
            pltpu.VMEM((1, OBS), jnp.int32),
            pltpu.VMEM((1, OBS), F32),
            pltpu.VMEM((1, OBS), F32),
            pltpu.SMEM((1, BINS), jnp.int32),
            pltpu.VMEM((OBS, K), F32),
            pltpu.VMEM((9 * K, OBS), BF16),
            pltpu.VMEM((OBS, 2 * K), BF16),
            pltpu.VMEM((9, GROWS, K), F32),
            pltpu.VMEM((2, 3, GROWS, K), F32),
            pltpu.VMEM((2, GROWS, K), F32),
            pltpu.VMEM((2, GROWS, K), F32),
            pltpu.VMEM((BLOCK, 1, K), F32),
            pltpu.VMEM((planes, 1, K), F32),
            pltpu.VMEM((3, 3, K, K), BF16),
            dma((LOADS,)),
            dma((5,)),
            dma((BLOCK,)),
            dma((BLOCK,)),
            dma((planes,)),
            dma((planes,)),
            dma((2,)),
            dma((2,)),
            dma((2,)),
            dma((2,)),
            dma((2,)),
            dma((2,)),
            dma((2,)),
            dma((2,)),
            dma((2, 2)),
            dma((2, 2)),
        ],
        compiler_params=pltpu.CompilerParams(
            collective_id=0, has_side_effects=True, vmem_limit_bytes=20 * 1024 * 1024
        ),
    )(
        pin(field),
        pin(cells),
        pin(obs_value.reshape(1, OBS)),
        pin(obs_inverse.reshape(1, OBS)),
        obs_count.reshape(1, 1),
        pin(taper.reshape(1, BINS)),
    )
    result = pl.pallas_call(
        last_pass,
        out_shape=jax.ShapeDtypeStruct((CELLS, K), BF16),
        in_specs=[vmem] * 4,
        out_specs=pl.BlockSpec(memory_space=pltpu.HBM),
        scratch_shapes=[pltpu.VMEM((CELLS, K), BF16), dma((CELLS // (8 * TY),))],
        compiler_params=pltpu.CompilerParams(vmem_limit_bytes=16 * 1024 * 1024),
    )(*parts)
    return result.reshape(levels, tile_x, tile_y, members)


def solution(mesh):
    in_specs = (
        P(None, "gx", "gy", None),
        P("gx", "gy", None),
        P("gx", "gy", None),
        P("gx", "gy", None),
        P("gx", "gy"),
        P(),
    )
    out_specs = P(None, "gx", "gy", None)
    step = functools.partial(local, mesh.shape["gx"], mesh.shape["gy"])
    return jax.shard_map(step, mesh=mesh, in_specs=in_specs, out_specs=out_specs, check_vma=False)
```

```python
import functools

import jax
import jax.numpy as jnp
from jax import lax
from jax.experimental import pallas as pl
from jax.experimental.pallas import tpu as pltpu
from jax.sharding import PartitionSpec as P

NSTEPS = 6
MESH = pl.DeviceIdType.MESH
F32 = jnp.float32
BF16 = jnp.bfloat16

K = 128
OBS = 512
TX = 64
TY = 128
BINS = 64
LIMIT = 9 * (TX * TX + TY * TY)
CELLS = 2 * TX * TY
LOADS = 8
GROWS = K + 8
BLOCK = 16


def nt(a, b):
    return lax.dot_general(a, b, (((1,), (1,)), ((), ())), preferred_element_type=F32)


def mm(a, b):
    return jnp.dot(a, b, preferred_element_type=F32)


def product3(a, b):
    a_top, b_top = a.astype(BF16), b.astype(BF16)
    a_rest = (a - a_top.astype(F32)).astype(BF16)
    b_rest = (b - b_top.astype(F32)).astype(BF16)
    return mm(
        jnp.concatenate([a_top, a_rest, a_top], axis=1),
        jnp.concatenate([b_top, b_top, b_rest], axis=0),
    )


def full_sum(x):
    return jnp.sum(jnp.sum(x, axis=0, keepdims=True), axis=1, keepdims=True)


def times(a, b):
    out = [None] * (len(a) + len(b) - 1)
    for i, x in enumerate(a):
        for j, y in enumerate(b):
            out[i + j] = x * y if out[i + j] is None else out[i + j] + x * y
    return out


def combine(coefficients, powers):
    total = coefficients[0] * powers[0]
    for coefficient, power in zip(coefficients[1:], powers[1:]):
        total = total + coefficient * power
    return total


def beta(position, has_low, has_high):
    low = 0.5 * ((1.0 - position) * (1.0 - position))
    middle = 0.5 + position - position * position
    top = 0.5 * (position * position)
    middle = middle + (1.0 - has_low) * low + (1.0 - has_high) * top
    return low * has_low, middle, top * has_high


def by_line(table, p, line, x):
    return (x.reshape(TY // 8, 8, K) * table[p, line][None]).reshape(TY, K)


def last_pass(acc, scaled, sides_w, bx_tab, out, result, out_sem):
    size = 8 * TY
    copies = [
        pltpu.make_async_copy(
            result.at[pl.ds(c * size, size), :], out.at[pl.ds(c * size, size), :], out_sem.at[c]
        )
        for c in range(CELLS // size)
    ]

    for c in range(CELLS // size):
        product = mm(scaled[c * size : (c + 1) * size, :], sides_w[...])
        for n in range(size // TY):
            line = (c * (size // TY) + n) % TX
            cut = slice(n * TY, (n + 1) * TY)
            at = slice(c * size + n * TY, c * size + (n + 1) * TY)
            result[at, :] = (
                acc[at, :]
                + by_line(bx_tab, 0, line, product[cut, :K])
                + by_line(bx_tab, 2, line, product[cut, K:])
            ).astype(BF16)
        copies[c].start()
    for copy in copies:
        copy.wait()


def kernel(
    n_gx,
    n_gy,
    field,
    cell_h,
    value_h,
    inverse_h,
    count,
    taper_h,
    acc,
    scaled,
    sides_w,
    bx_tab,
    field_v,
    s_own,
    u_side,
    by_tab,
    cell_s,
    cell_v,
    value,
    inverse,
    taper,
    picked,
    weighted,
    rhs,
    gram,
    gram_x,
    half,
    gram_y,
    sum_a,
    sum_b,
    w_all,
    load_sem,
    small_sem,
    send_a,
    recv_a,
    send_b,
    recv_b,
    send_gx,
    recv_gx,
    send_gy,
    recv_gy,
    send_wy,
    recv_wy,
    send_wx,
    recv_wx,
    send_wc,
    recv_wc,
):
    gx = lax.axis_index("gx")
    gy = lax.axis_index("gy")
    span = CELLS // LOADS
    loads = [
        pltpu.make_async_copy(
            field.at[pl.ds(k * span, span), :], field_v.at[pl.ds(k * span, span), :], load_sem.at[k]
        )
        for k in range(LOADS)
    ]
    small = [
        pltpu.make_async_copy(source, target, small_sem.at[k])
        for k, (source, target) in enumerate(
            (
                (cell_h, cell_v),
                (taper_h, taper),
                (inverse_h, inverse),
                (value_h, value),
                (cell_h, cell_s),
            )
        )
    ]
    for copy in small + loads:
        copy.start()

    gram_x[...] = jnp.zeros_like(gram_x)
    gram_y[...] = jnp.zeros_like(gram_y)
    w_all[...] = jnp.zeros_like(w_all)

    block = lax.div(gx, BLOCK)
    lane = lax.rem(gx, BLOCK)
    plane = block * n_gy + gy
    planes = n_gx // BLOCK * n_gy

    def ring_peer(k):
        return (block * BLOCK + lax.rem(lane + k, BLOCK), gy)

    def plane_peer(k):
        other = lax.rem(plane + k, planes)
        return (lax.div(other, n_gy) * BLOCK + lane, lax.rem(other, n_gy))

    west, east = gx > 0, gx < n_gx - 1
    south, north = gy > 0, gy < n_gy - 1
    sides = [
        (west, (gx - 1, gy)),
        (east, (gx + 1, gy)),
        (south, (gx, gy - 1)),
        (north, (gx, gy + 1)),
        (jnp.logical_and(west, south), (gx - 1, gy - 1)),
        (jnp.logical_and(west, north), (gx - 1, gy + 1)),
        (jnp.logical_and(east, south), (gx + 1, gy - 1)),
        (jnp.logical_and(east, north), (gx + 1, gy + 1)),
    ]

    barrier = pltpu.get_barrier_semaphore()
    for k in range(1, BLOCK):
        pl.semaphore_signal(barrier, inc=1, device_id=ring_peer(k), device_id_type=MESH)
    for k in range(1, planes):
        pl.semaphore_signal(barrier, inc=1, device_id=plane_peer(k), device_id_type=MESH)
    for there, peer in sides:

        @pl.when(there)
        def _(peer=peer):
            pl.semaphore_signal(barrier, inc=1, device_id=peer, device_id_type=MESH)

    has_s, has_n = south.astype(F32), north.astype(F32)
    has_w, has_e = west.astype(F32), east.astype(F32)
    v_pos = (lax.broadcasted_iota(jnp.int32, (TY, K), 0).astype(F32) + 0.5) / TY
    for q, part in enumerate(beta(v_pos, has_s, has_n)):
        by_tab[q] = part

    u_pos = (lax.broadcasted_iota(jnp.int32, (TX, 8, K), 0).astype(F32) + 0.5) / TX
    for p, part in enumerate(beta(u_pos, has_w, has_e)):
        bx_tab[p] = part

    for copy in small:
        copy.wait()

    cells = cell_v[...]
    col = lax.shift_right_logical(cells & (TX * TY - 1), 7)
    row = cells & (TY - 1)
    slot = lax.broadcasted_iota(jnp.int32, (1, OBS), 1)
    live = (slot < count[0, 0]).astype(F32)
    weight = (inverse[...] * live).astype(BF16).astype(F32)
    which = lax.broadcasted_iota(jnp.int32, (BLOCK, OBS), 0)
    third = lax.shift_right_logical(which * 11, 5)
    dx = 2 * ((third - 1) * TX + col) - (TX - 1)
    dy = 2 * ((which - third * 3 - 1) * TY + row) - (TY - 1)
    distance = (dx * dx + dy * dy) * BINS
    factor = jnp.zeros((BLOCK, OBS), F32)
    for n in range(BINS):
        factor = jnp.where(distance >= n * LIMIT, taper[0, n].astype(F32), factor)
    effective = weight * (factor / 1024.0)

    for k in range(LOADS):
        loads[k].wait()

        def widen(i, _, k=k):
            rows = pl.ds(pl.multiple_of(k * span + i * 256, 256), 256)
            acc[rows, :] = field_v[rows, :].astype(F32)
            return 0

        lax.fori_loop(0, span // 256, widen, 0, unroll=True)

    def pick(i, _):
        for k in range(16):
            s = i * 16 + k
            picked[pl.ds(s, 1), :] = acc[pl.ds(cell_s[0, s], 1), :]
        return 0

    lax.fori_loop(0, OBS // 16, pick, 0)

    mean = jnp.full((K, K), 1.0 / K, BF16)
    cols = lax.broadcasted_iota(jnp.int32, (K, K), 1)
    rows_ = lax.broadcasted_iota(jnp.int32, (K, K), 0)
    eye = (cols == rows_).astype(F32)
    chosen = picked[...]
    chosen_b = chosen.astype(BF16)
    center_b = mm(chosen_b, mean)
    center_r = nt(mean[:16], chosen_b)[:1]
    perturb = (chosen - center_b).astype(BF16)
    perturb_t = nt(eye.astype(BF16), perturb)
    innovation = (value[...] - center_r).astype(BF16).astype(F32)
    spread = jnp.sum(perturb_t * perturb_t, axis=0, keepdims=True) / (K - 1)
    num = weight * innovation * innovation
    den = weight * spread + live
    num = num[:, :K] + num[:, K : 2 * K] + num[:, 2 * K : 3 * K] + num[:, 3 * K :]
    den = den[:, :K] + den[:, K : 2 * K] + den[:, 2 * K : 3 * K] + den[:, 3 * K :]
    num = num + pltpu.roll(num, K // 2, 1)
    den = den + pltpu.roll(den, K // 2, 1)
    lanes = lax.broadcasted_iota(jnp.int32, (1, K), 1)
    sum_a[0] = jnp.where(lanes < K // 2, num, den)

    pl.semaphore_wait(
        barrier,
        BLOCK - 1
        + planes - 1
        + sum(there.astype(jnp.int32) for there, _ in sides),
    )

    def remote(src, dst, send, recv, peer):
        return pltpu.make_async_remote_copy(
            src_ref=src, dst_ref=dst, send_sem=send, recv_sem=recv, device_id=peer, device_id_type=MESH
        )

    ring = [
        remote(sum_a.at[0], sum_a.at[k], send_a.at[k], recv_a.at[k], ring_peer(k))
        for k in range(1, BLOCK)
    ]
    for copy in ring:
        copy.start()

    rhs[:, :K] = perturb
    d_rows = jnp.broadcast_to(innovation, (K, OBS)).T
    rhs[:, K:] = d_rows.astype(BF16)
    def for_sides(pairs, act):
        for there, copy in pairs:

            @pl.when(there)
            def _(copy=copy):
                act(copy)

    gx_out = []
    gx_in = []
    for q in (0, 2, 1):
        to_e = remote(gram.at[q], gram_x.at[0, q], send_gx.at[0, q], recv_gx.at[0, q], (gx + 1, gy))
        to_w = remote(gram.at[6 + q], gram_x.at[1, q], send_gx.at[1, q], recv_gx.at[1, q], (gx - 1, gy))
        gx_out += [(east, to_e), (west, to_w)]
        gx_in += [(west, to_e), (east, to_w)]

    right = rhs[...]
    for n, t in enumerate((0, 6, 2, 8, 1, 7, 3, 5, 4)):
        weighted[t * K : (t + 1) * K, :] = (perturb_t * effective[t : t + 1, :]).astype(BF16)
        product = mm(weighted[t * K : (t + 1) * K, :], right)
        gram[t, :K, :] = product[:, :K]
        gram[t, K:, :] = jnp.broadcast_to(
            jnp.sum(product[:, K:] * eye, axis=0, keepdims=True), (GROWS - K, K)
        )
        if n < 6 and n % 2 == 1:
            for_sides(gx_out[n - 1 : n + 1], lambda copy: copy.start())

    lines = 8

    def prepare(c, _):
        size = lines * TY
        rows = pl.ds(pl.multiple_of(c * size, size), size)
        members = field_v[rows, :]
        center = mm(members, mean)
        acc[rows, :] = center
        deviation = members.astype(F32) - center
        low, middle, top = by_tab[0], by_tab[1], by_tab[2]
        for n in range(lines):
            line = (c * lines + n) & (TX - 1)
            piece = deviation[n * TY : (n + 1) * TY]
            at = pl.ds(pl.multiple_of(c * size + n * TY, TY), TY)
            scaled[at, :K] = (piece * low).astype(BF16)
            scaled[at, K : 2 * K] = (piece * middle).astype(BF16)
            scaled[at, 2 * K :] = (piece * top).astype(BF16)
            s_own[at, :] = (piece * by_line(bx_tab, 1, line, middle)).astype(BF16)
            u_side[at, :] = by_line(bx_tab, 1, line, piece).astype(BF16)
        return 0

    steps = 2 * TX // lines
    lax.fori_loop(0, steps // 2, prepare, 0, unroll=True)

    for copy in ring:
        copy.wait_recv()
    sum_b[0] = jnp.sum(sum_a[...], axis=0)
    cross = [
        remote(sum_b.at[0], sum_b.at[k], send_b.at[k], recv_b.at[k], plane_peer(k))
        for k in range(1, planes)
    ]
    for copy in cross:
        copy.start()

    gy_out = [
        (north, remote(half.at[0], gram_y.at[0], send_gy.at[0], recv_gy.at[0], (gx, gy + 1))),
        (south, remote(half.at[1], gram_y.at[1], send_gy.at[1], recv_gy.at[1], (gx, gy - 1))),
    ]
    gy_in = [(south, gy_out[0][1]), (north, gy_out[1][1])]
    for n, q in enumerate((0, 2)):
        for_sides(gx_in[2 * n : 2 * n + 2], lambda copy: copy.wait_recv())
        half[n] = gram[3 + q] + gram_x[0, q] + gram_x[1, q]
        for_sides(gy_out[n : n + 1], lambda copy: copy.start())

    lax.fori_loop(steps // 2, steps, prepare, 0, unroll=True)

    for_sides(gx_in[4:] + gy_in, lambda copy: copy.wait_recv())
    total = gram[4] + gram_x[0, 1] + gram_x[1, 1] + gram_y[0] + gram_y[1]
    projected = jnp.broadcast_to(total[K : K + 1], (K, K)).T
    total = total[:K] / (K - 1)
    square = full_sum(total * total)
    trace = full_sum(total * eye)
    size_g = jnp.maximum(jnp.sqrt(square), 1e-20)
    p1 = total / size_g
    p2 = product3(p1, p1)
    both = product3(p2, jnp.concatenate([p1, p2], axis=1))
    p3, p4 = both[:, :K], both[:, K:]
    p5 = product3(p2, p3)
    powers = (eye, p1, p2, p3, p4, p5)

    for copy in cross:
        copy.wait_recv()
    sums = jnp.sum(sum_b[...], axis=0)
    numerator = jnp.sum(jnp.where(lanes < K // 2, sums, 0.0), axis=1, keepdims=True)
    denominator = jnp.sum(jnp.where(lanes < K // 2, 0.0, sums), axis=1, keepdims=True)
    inflation = numerator / denominator

    shrink = 1.0 / inflation
    frob = jnp.sqrt(K * shrink * shrink + 2.0 * shrink * trace + square)
    root_c = [shrink / frob, size_g / frob]
    inv_c = None
    for sweep in range(2):
        joint_c = root_c if sweep == 0 else times(inv_c, root_c)
        step_c = [-0.5 * x for x in joint_c]
        step_c[0] = step_c[0] + 1.5
        inv_c = step_c if sweep == 0 else times(step_c, inv_c)
        root_c = times(root_c, step_c)
    root = combine(root_c, powers)
    inv_root = combine(inv_c, powers)
    for sweep in range(2, NSTEPS - 1):
        correction = 1.5 * eye - 0.5 * product3(inv_root, root)
        both = product3(correction, jnp.concatenate([root, inv_root], axis=1))
        root, inv_root = both[:, :K], both[:, K:]
    both = product3(inv_root, jnp.concatenate([root, projected], axis=1))
    correction = 1.5 * eye - 0.5 * both[:, :K]
    both = product3(correction, jnp.concatenate([inv_root, both[:, K:]], axis=1))
    inv_root = both[:, :K]
    shift = product3(inv_root, both[:, K:]) / (frob * (K - 1))
    w_all[1, 1] = (inv_root / jnp.sqrt(frob) + shift).astype(BF16)

    mine = w_all.at[1, 1]
    wy_out = [
        (north, remote(mine, w_all.at[1, 0], send_wy.at[0], recv_wy.at[0], (gx, gy + 1))),
        (south, remote(mine, w_all.at[1, 2], send_wy.at[1], recv_wy.at[1], (gx, gy - 1))),
    ]
    wy_in = [(south, wy_out[0][1]), (north, wy_out[1][1])]
    wx_out = [
        (east, remote(mine, w_all.at[0, 1], send_wx.at[0], recv_wx.at[0], (gx + 1, gy))),
        (west, remote(mine, w_all.at[2, 1], send_wx.at[1], recv_wx.at[1], (gx - 1, gy))),
    ]
    wx_in = [(west, wx_out[0][1]), (east, wx_out[1][1])]
    for_sides(wy_out, lambda copy: copy.start())
    for_sides(wx_out, lambda copy: copy.start())
    wc_out = []
    wc_in = []
    for n, (up, down, q) in enumerate(((north, south, 0), (south, north, 2))):
        row = gy + 1 if q == 0 else gy - 1
        to_e = remote(mine, w_all.at[0, q], send_wc.at[0, n], recv_wc.at[0, n], (gx + 1, row))
        to_w = remote(mine, w_all.at[2, q], send_wc.at[1, n], recv_wc.at[1, n], (gx - 1, row))
        wc_out += [(jnp.logical_and(up, east), to_e), (jnp.logical_and(up, west), to_w)]
        wc_in += [(jnp.logical_and(down, west), to_e), (jnp.logical_and(down, east), to_w)]
    for_sides(wc_out, lambda copy: copy.start())

    size = 16 * TY

    def own(c, _):
        rows = pl.ds(pl.multiple_of(c * size, size), size)
        acc[rows, :] = acc[rows, :] + mm(s_own[rows, :], w_all[1, 1])
        return 0

    lax.fori_loop(0, CELLS // size, own, 0, unroll=True)

    for_sides(wy_in, lambda copy: copy.wait_recv())

    def along_gy(c, _):
        rows = pl.ds(pl.multiple_of(c * size, size), size)
        product = mm(u_side[rows, :], jnp.concatenate([w_all[1, 0], w_all[1, 2]], axis=1))
        low, top = by_tab[0], by_tab[2]
        for n in range(size // TY):
            cut = slice(n * TY, (n + 1) * TY)
            at = pl.ds(pl.multiple_of(c * size + n * TY, TY), TY)
            acc[at, :] = acc[at, :] + (low * product[cut, :K] + top * product[cut, K:])
        return 0

    lax.fori_loop(0, CELLS // size, along_gy, 0, unroll=True)

    for_sides(wx_in, lambda copy: copy.wait_recv())
    for_sides(wc_in, lambda copy: copy.wait_recv())
    for q in range(3):
        sides_w[q * K : (q + 1) * K, :K] = w_all[0, q]
        sides_w[q * K : (q + 1) * K, K:] = w_all[2, q]

    for copy in ring + cross:
        copy.wait_send()
    for_sides(gx_out + gy_out + wy_out + wx_out + wc_out, lambda copy: copy.wait_send())


def local(n_gx, n_gy, background, cell_index, obs_value, obs_inverse, obs_count, taper):
    levels, tile_x, tile_y, members = background.shape
    field = background.reshape(-1, members)
    cells = cell_index.reshape(1, OBS)
    vmem = pl.BlockSpec(memory_space=pltpu.VMEM)
    hbm = pl.BlockSpec(memory_space=pltpu.HBM)
    dma = pltpu.SemaphoreType.DMA
    planes = n_gx // BLOCK * n_gy
    pin = functools.partial(pltpu.with_memory_space_constraint, memory_space=pltpu.HBM)
    parts = pl.pallas_call(
        functools.partial(kernel, n_gx, n_gy),
        out_shape=(
            pltpu.VMEM((CELLS, K), F32),
            pltpu.VMEM((CELLS, 3 * K), BF16),
            pltpu.VMEM((3 * K, 2 * K), BF16),
            pltpu.VMEM((3, TX, 8, K), F32),
        ),
        in_specs=[hbm, hbm, hbm, hbm, pl.BlockSpec(memory_space=pltpu.SMEM), hbm],
        out_specs=(vmem, vmem, vmem, vmem),
        scratch_shapes=[
            pltpu.VMEM((CELLS, K), BF16),
            pltpu.VMEM((CELLS, K), BF16),
            pltpu.VMEM((CELLS, K), BF16),
            pltpu.VMEM((3, TY, K), F32),
            pltpu.SMEM((1, OBS), jnp.int32),
            pltpu.VMEM((1, OBS), jnp.int32),
            pltpu.VMEM((1, OBS), F32),
            pltpu.VMEM((1, OBS), F32),
            pltpu.SMEM((1, BINS), jnp.int32),
            pltpu.VMEM((OBS, K), F32),
            pltpu.VMEM((9 * K, OBS), BF16),
            pltpu.VMEM((OBS, 2 * K), BF16),
            pltpu.VMEM((9, GROWS, K), F32),
            pltpu.VMEM((2, 3, GROWS, K), F32),
            pltpu.VMEM((2, GROWS, K), F32),
            pltpu.VMEM((2, GROWS, K), F32),
            pltpu.VMEM((BLOCK, 1, K), F32),
            pltpu.VMEM((planes, 1, K), F32),
            pltpu.VMEM((3, 3, K, K), BF16),
            dma((LOADS,)),
            dma((5,)),
            dma((BLOCK,)),
            dma((BLOCK,)),
            dma((planes,)),
            dma((planes,)),
            dma((2, 3)),
            dma((2, 3)),
            dma((2,)),
            dma((2,)),
            dma((2,)),
            dma((2,)),
            dma((2,)),
            dma((2,)),
            dma((2, 2)),
            dma((2, 2)),
        ],
        compiler_params=pltpu.CompilerParams(
            collective_id=0, has_side_effects=True, vmem_limit_bytes=20 * 1024 * 1024
        ),
    )(
        pin(field),
        pin(cells),
        pin(obs_value.reshape(1, OBS)),
        pin(obs_inverse.reshape(1, OBS)),
        obs_count.reshape(1, 1),
        pin(taper.reshape(1, BINS)),
    )
    result = pl.pallas_call(
        last_pass,
        out_shape=jax.ShapeDtypeStruct((CELLS, K), BF16),
        in_specs=[vmem] * 4,
        out_specs=pl.BlockSpec(memory_space=pltpu.HBM),
        scratch_shapes=[pltpu.VMEM((CELLS, K), BF16), dma((CELLS // (8 * TY),))],
        compiler_params=pltpu.CompilerParams(vmem_limit_bytes=16 * 1024 * 1024),
    )(*parts)
    return result.reshape(levels, tile_x, tile_y, members)


def solution(mesh):
    in_specs = (
        P(None, "gx", "gy", None),
        P("gx", "gy", None),
        P("gx", "gy", None),
        P("gx", "gy", None),
        P("gx", "gy"),
        P(),
    )
    out_specs = P(None, "gx", "gy", None)
    step = functools.partial(local, mesh.shape["gx"], mesh.shape["gy"])
    return jax.shard_map(step, mesh=mesh, in_specs=in_specs, out_specs=out_specs, check_vma=False)
```
